32 devices in a mesh: gx: 8 (over y, x, core), gy: 4 (over z).
Axes of the slice: x: 2, y: 2, z: 4, core: 2. Of those that a mesh axis runs over, the one named last changes fastest.
Arguments:
- cells: bfloat16 [1024, 256, 128], P('gx', 'gy'), may hold values from -6 to 6
- cotangent: bfloat16 [1024, 256, 128], P('gx', 'gy'), may hold values from -6 to 6
- lift_weight: bfloat16 [128, 512], replicated, may hold values from -0.5 to 0.5
- drop_weight: bfloat16 [512, 128], replicated, may hold values from -0.25 to 0.25
- xmode_weight: bfloat16 [2, 16, 128, 128], P(None, 'gx'), may hold values from -0.375 to 0.375
- ymode_weight: bfloat16 [2, 8, 128, 128], replicated, may hold values from -0.375 to 0.375
- coarse_weight: bfloat16 [128, 128], replicated, may hold values from -0.5 to 0.5
- coarse_mix: bfloat16 [16, 16], replicated, may hold values from -1.5 to 1.5
Outputs:
- cell_grad: bfloat16 [1024, 256, 128], P('gx', 'gy')
- lift_grad: float32 [128, 512], replicated
- drop_grad: float32 [512, 128], replicated
- xmode_grad: float32 [2, 16, 128, 128], P(None, 'gx')
- ymode_grad: float32 [2, 8, 128, 128], replicated
- coarse_weight_grad: float32 [128, 128], replicated
- coarse_mix_grad: float32 [16, 16], replicated
The draws below stay inside these ranges and needn't reach their ends.
All inputs are finite; a program needn't handle non-finite values.
Results may differ from the reference program's by a relative error of at most 0.006.
Values sent between devices are 32-bit elements; how exact they have to be, the bound alone decides.
A program may use at most 128 MiB of HBM per device.

```python
import math
import jax
import jax.numpy as jnp
from jax import lax

WIDTH = 128
FFN_WIDTH = 512
MODES_X = 16
MODES_Y = 8
POOL = 16
NX = 1024
NY = 256
NYC = 16


def level_of(own_key, dims, shards, least, high):
    def one(position, shards_of):
        draws = jax.random.uniform(jax.random.fold_in(jax.random.fold_in(own_key, 6), position), (shards_of,), jnp.float32, least / len(shards), high / len(shards))
        return jnp.repeat(jnp.exp(draws), dims[position] // shards_of).reshape((-1,) + (1,) * (len(dims) - position - 1))

    gain = one(*shards[0])
    for cut in shards[1:]:
        gain = gain * one(*cut)
    return gain


def gaussian(rng, shape, deviation, bound, pieces=(), kind=jnp.bfloat16):
    result = deviation * jax.random.normal(rng, shape, jnp.float32)
    if pieces:
        result = result * level_of(rng, shape, pieces, -0.22, 0.18)
    return jnp.clip(result, -bound, bound).astype(kind)


def setup_inputs(seed: int = 0) -> dict:
    seeds = jax.random.split(jax.random.key(seed), 9)
    cells = gaussian(seeds[0], (NX, NY, WIDTH), 1.0, 6.0, ((0, 8), (1, 4)))
    cotangent = gaussian(seeds[1], (NX, NY, WIDTH), 1.0, 6.0, ((0, 8), (1, 4)))
    lift_weight = gaussian(seeds[2], (WIDTH, FFN_WIDTH), WIDTH ** -0.5, 0.5)
    drop_weight = gaussian(seeds[3], (FFN_WIDTH, WIDTH), FFN_WIDTH ** -0.5, 0.25)
    xmode_weight = gaussian(seeds[4], (2, MODES_X, WIDTH, WIDTH), (2 * WIDTH) ** -0.5, 0.375, ((1, 8),))
    ymode_weight = gaussian(seeds[5], (2, MODES_Y, WIDTH, WIDTH), (2 * WIDTH) ** -0.5, 0.375)
    coarse_weight = gaussian(seeds[6], (WIDTH, WIDTH), WIDTH ** -0.5, 0.5)
    coarse_mix = gaussian(seeds[7], (NYC, NYC), NYC ** -0.5, 1.5)
    return dict(cells=cells, cotangent=cotangent, lift_weight=lift_weight, drop_weight=drop_weight, xmode_weight=xmode_weight, ymode_weight=ymode_weight, coarse_weight=coarse_weight, coarse_mix=coarse_mix)


gelu_scale = 0.7978845608028654
gelu_cubic = 0.044715
highest = lax.Precision.HIGHEST

def gelu_value(values):
    tangent = jnp.tanh(gelu_scale * (values + gelu_cubic * values * values * values))
    return 0.5 * values * (1.0 + tangent)

def gelu_slope(values):
    tangent = jnp.tanh(gelu_scale * (values + gelu_cubic * values * values * values))
    return 0.5 * (1.0 + tangent) + 0.5 * values * (1.0 - tangent * tangent) * gelu_scale * (1.0 + 3.0 * gelu_cubic * values * values)

def mode_basis(mode_count, length, offset, extent):
    frequency = jnp.arange(mode_count, dtype=jnp.int32)
    places = offset + jnp.arange(extent, dtype=jnp.int32)
    phase_index = frequency[:, None] * places[None, :] % length
    angles = phase_index.astype(jnp.float32) * (2.0 * math.pi / length)
    return jnp.concatenate([jnp.cos(angles), -jnp.sin(angles)], axis=0)

def mix_modes(spectrum, weights):

    def product(former, latter):
        return jnp.einsum('mrc,mcd->mrd', former, latter, precision=highest)
    real_out = product(spectrum[0], weights[0]) - product(spectrum[1], weights[1])
    imaginary_out = product(spectrum[0], weights[1]) + product(spectrum[1], weights[0])
    return jnp.stack([real_out, imaginary_out])

def mix_back(spectrum, gradient, weights):

    def contract_cells(former, latter):
        return jnp.einsum('mrc,mrd->mcd', former, latter, precision=highest)

    def contract_channels(former, latter):
        return jnp.einsum('mrd,mcd->mrc', former, latter, precision=highest)
    weight_real = contract_cells(spectrum[0], gradient[0]) + contract_cells(spectrum[1], gradient[1])
    weight_imaginary = contract_cells(spectrum[0], gradient[1]) - contract_cells(spectrum[1], gradient[0])
    spec_real = contract_channels(gradient[0], weights[0]) + contract_channels(gradient[1], weights[1])
    spec_imaginary = contract_channels(gradient[1], weights[0]) - contract_channels(gradient[0], weights[1])
    return (jnp.stack([weight_real, weight_imaginary]), jnp.stack([spec_real, spec_imaginary]))

def reference(cells, cotangent, lift_weight, drop_weight, xmode_weight, ymode_weight, coarse_weight, coarse_mix):
    block_count = NX // POOL
    row_basis = mode_basis(MODES_X, NX, 0, NX)
    column_basis = mode_basis(MODES_Y, NY, 0, NY)
    column_basis_low = column_basis.astype(jnp.bfloat16).astype(jnp.float32)
    row_weight = xmode_weight.astype(jnp.float32)
    column_weight = ymode_weight.astype(jnp.float32)
    coarse_float = coarse_weight.astype(jnp.float32)
    mixing_float = coarse_mix.astype(jnp.float32)
    row_spec = jnp.dot(row_basis.astype(jnp.bfloat16), cells.reshape(NX, NY * WIDTH), preferred_element_type=jnp.float32) * (1.0 / math.sqrt(NX))
    row_spec = row_spec.reshape(2, MODES_X, NY, WIDTH)
    row_mixed = mix_modes(row_spec, row_weight).reshape(2 * MODES_X, NY * WIDTH)
    cell_blocks = cells.reshape(block_count, POOL, NY, WIDTH)
    cotangent_blocks = cotangent.reshape(block_count, POOL, NY, WIDTH)
    block_ids = jnp.arange(block_count, dtype=jnp.int32)

    def first_pass(cell_block):
        widened = cell_block.astype(jnp.float32)
        spectrum = jnp.einsum('ry,xyc->rxc', column_basis_low, widened, precision=highest)
        pooled_row = widened.reshape(POOL, NYC, POOL, WIDTH).sum(axis=(0, 2)) / POOL
        return (spectrum, pooled_row)
    column_blocks, pooled = lax.map(first_pass, cell_blocks)
    column_spec = column_blocks.transpose(1, 0, 2, 3).reshape(2, MODES_Y, NX, WIDTH) * (1.0 / math.sqrt(NY))
    column_mixed = mix_modes(column_spec, column_weight).reshape(2 * MODES_Y, NX, WIDTH)
    coarse_pre = jnp.einsum('ijc,cd->ijd', pooled, coarse_float, precision=highest)
    coarse_act = gelu_value(coarse_pre)
    coarse_out = jnp.einsum('jk,ikc->ijc', mixing_float, coarse_act, precision=highest)

    def second_pass(totals, inputs):
        lift_total, drop_total, row_total = totals
        block_index, cotangent_block = inputs
        row_offset = block_index * POOL
        basis_rows = lax.dynamic_slice_in_dim(row_basis, row_offset, POOL, 1)
        row_field = jnp.dot(basis_rows.T, row_mixed, precision=highest) * (1.0 / math.sqrt(MODES_X))
        column_rows = lax.dynamic_slice_in_dim(column_mixed, row_offset, POOL, 1)
        column_field = jnp.einsum('ry,rxc->xyc', column_basis, column_rows, precision=highest) * (1.0 / math.sqrt(MODES_Y))
        coarse_row = lax.dynamic_slice_in_dim(coarse_out, block_index, 1, 0)
        lifted = jnp.broadcast_to(coarse_row[:, :, None, :], (1, NYC, POOL, WIDTH)).reshape(1, NY, WIDTH)
        summed = row_field.reshape(POOL, NY, WIDTH) + column_field + lifted
        ffn_input = summed.reshape(POOL * NY, WIDTH).astype(jnp.bfloat16)
        hidden_before = jnp.dot(ffn_input, lift_weight, preferred_element_type=jnp.float32)
        hidden_after = gelu_value(hidden_before).astype(jnp.bfloat16)
        cotangent_rows = cotangent_block.reshape(POOL * NY, WIDTH)
        drop_total = drop_total + jnp.dot(hidden_after.T, cotangent_rows, preferred_element_type=jnp.float32)
        after_grad = jnp.dot(cotangent_rows, drop_weight.T, preferred_element_type=jnp.float32)
        before_grad = (after_grad * gelu_slope(hidden_before)).astype(jnp.bfloat16)
        lift_total = lift_total + jnp.dot(ffn_input.T, before_grad, preferred_element_type=jnp.float32)
        summed_grad = jnp.dot(before_grad, lift_weight.T, preferred_element_type=jnp.float32).reshape(POOL, NY, WIDTH)
        row_total = row_total + jnp.dot(basis_rows, summed_grad.reshape(POOL, NY * WIDTH), precision=highest)
        column_piece = jnp.einsum('ry,xyc->rxc', column_basis, summed_grad, precision=highest)
        coarse_piece = summed_grad.reshape(POOL, NYC, POOL, WIDTH).sum(axis=(0, 2))
        return ((lift_total, drop_total, row_total), (column_piece, coarse_piece))
    initial = (jnp.zeros((WIDTH, FFN_WIDTH), jnp.float32), jnp.zeros((FFN_WIDTH, WIDTH), jnp.float32), jnp.zeros((2 * MODES_X, NY * WIDTH), jnp.float32))
    (lift_grad, drop_grad, row_sum), (column_pieces, coarse_grad) = lax.scan(second_pass, initial, (block_ids, cotangent_blocks))
    row_back = row_sum.reshape(2, MODES_X, NY, WIDTH) * (1.0 / math.sqrt(MODES_X))
    column_back = column_pieces.transpose(1, 0, 2, 3).reshape(2, MODES_Y, NX, WIDTH) * (1.0 / math.sqrt(MODES_Y))
    xmode_grad, row_spec_grad = mix_back(row_spec, row_back, row_weight)
    ymode_grad, column_spec_grad = mix_back(column_spec, column_back, column_weight)
    coarse_act_grad = jnp.einsum('jk,ijc->ikc', mixing_float, coarse_grad, precision=highest)
    coarse_mix_grad = jnp.einsum('ijc,ikc->jk', coarse_grad, coarse_act, precision=highest)
    coarse_pre_grad = coarse_act_grad * gelu_slope(coarse_pre)
    coarse_weight_grad = jnp.einsum('ijc,ijd->cd', pooled, coarse_pre_grad, precision=highest)
    pooled_grad = jnp.einsum('ijd,cd->ijc', coarse_pre_grad, coarse_float, precision=highest) * (1.0 / POOL)
    row_flat = row_spec_grad.reshape(2 * MODES_X, NY * WIDTH)
    column_flat = column_spec_grad.reshape(2 * MODES_Y, NX, WIDTH)

    def third_pass(inputs):
        block_index, cotangent_block = inputs
        row_offset = block_index * POOL
        basis_rows = lax.dynamic_slice_in_dim(row_basis, row_offset, POOL, 1)
        row_piece = jnp.dot(basis_rows.T, row_flat, precision=highest).reshape(POOL, NY, WIDTH) * (1.0 / math.sqrt(NX))
        column_rows = lax.dynamic_slice_in_dim(column_flat, row_offset, POOL, 1)
        column_piece = jnp.einsum('ry,rxc->xyc', column_basis, column_rows, precision=highest) * (1.0 / math.sqrt(NY))
        pooled_row = lax.dynamic_slice_in_dim(pooled_grad, block_index, 1, 0)
        lifted = jnp.broadcast_to(pooled_row[:, :, None, :], (1, NYC, POOL, WIDTH)).reshape(1, NY, WIDTH)
        return (cotangent_block.astype(jnp.float32) + row_piece + column_piece + lifted).astype(jnp.bfloat16)
    cell_grad = lax.map(third_pass, (block_ids, cotangent_blocks)).reshape(NX, NY, WIDTH)
    return (cell_grad, lift_grad, drop_grad, xmode_grad, ymode_grad, coarse_weight_grad, coarse_mix_grad)
```

```python
import functools
import math

import jax
import jax.numpy as jnp
import numpy as np
from jax import lax
from jax.experimental import pallas as pl
from jax.experimental.pallas import tpu as pltpu
from jax.sharding import PartitionSpec as P

MODES_X = 16
MODES_Y = 8
POOL = 16
TILE = 8

gelu_scale = 0.7978845608028654
gelu_cubic = 0.044715
MESH = pl.DeviceIdType.MESH
VMEM_SPEC = pl.BlockSpec(memory_space=pltpu.VMEM)
low = jnp.bfloat16
wide = jnp.float32


def gelu_pair(values):
    square = values * values
    tangent = jnp.tanh(values * (gelu_scale + (gelu_scale * gelu_cubic) * square))
    half = 0.5 + 0.5 * tangent
    bend = values * (0.5 * gelu_scale + (1.5 * gelu_scale * gelu_cubic) * square)
    return values * half, half + bend * (1.0 - tangent * tangent)


def dot(former, latter):
    return jnp.dot(former, latter, preferred_element_type=wide)


def dot_nt(former, latter):
    return lax.dot_general(former, latter, (((1,), (1,)), ((), ())), preferred_element_type=wide)


def dot_tn(former, latter):
    return lax.dot_general(former, latter, (((0,), (0,)), ((), ())), preferred_element_type=wide)


def basis_table(mode_count, length):
    phase = np.outer(np.arange(mode_count), np.arange(length)) % length
    angles = phase * (2.0 * math.pi / length)
    return np.concatenate([np.cos(angles), -np.sin(angles)], axis=0).astype(np.float32)


def analyse(block, first, step, xback_ref, yback_ref, row_ref, column_ref, pool_ref):
    rows, columns, channels = block.shape
    for tile in range(columns // TILE):
        own = pl.ds(tile * TILE, TILE)
        piece = block[:, tile * TILE : (tile + 1) * TILE, :].reshape(rows * TILE, channels)
        part = dot(xback_ref[...], piece.astype(low)).reshape(2 * MODES_X, TILE, channels)

        @pl.when(first)
        def _():
            row_ref[:, own, :] = part

        @pl.when(jnp.logical_not(first))
        def _():
            row_ref[:, own, :] += part

    for tile in range(rows // TILE):
        piece = block[tile * TILE : (tile + 1) * TILE].reshape(TILE * columns, channels)
        part = dot(yback_ref[...], piece.astype(low))
        column_ref[:, tile * TILE : (tile + 1) * TILE, :] = part.reshape(
            2 * MODES_Y, TILE, channels
        )
    pooled = block.sum(axis=0).reshape(columns // POOL, POOL, channels).sum(axis=1)
    pool_ref[:, pl.ds(step, 1), :] = pooled[:, None, :]


def analysis_kernel(cells_ref, xback_ref, yback_ref, row_ref, column_ref, pool_ref):
    step = pl.program_id(0)
    block = cells_ref[...].astype(wide)
    analyse(block, step == 0, step, xback_ref, yback_ref, row_ref, column_ref, pool_ref)


def synthesise(rows, columns, channels, xfore, yfore_ref, row_low, column_of, coarse_of):
    parts = []
    for tile in range(rows // TILE):
        modes = column_of(tile).reshape(2 * MODES_Y * TILE, channels).astype(low)
        parts.append(dot(yfore_ref[...], modes).reshape(TILE, columns, channels))
    field = jnp.concatenate(parts, axis=0)
    pieces = []
    for tile in range(columns // TILE):
        part = dot(xfore, row_low(tile)).reshape(rows, TILE, channels)
        pieces.append(part + coarse_of(tile * TILE // POOL))
    return field + jnp.concatenate(pieces, axis=1)


def ffn_kernel(
    cotangent_ref,
    rowf_ref,
    colf_ref,
    coarse_ref,
    lift_ref,
    liftt_ref,
    dropt_ref,
    xfore_ref,
    xback_ref,
    yfore_ref,
    yback_ref,
    row_ref,
    column_ref,
    pool_ref,
    total_ref,
    rowlow_ref,
):
    step = pl.program_id(0)
    rows, columns, channels = cotangent_ref.shape
    hidden = lift_ref.shape[1]

    @pl.when(step == 0)
    def _():
        for tile in range(columns // TILE):
            rowlow_ref[tile] = (
                rowf_ref[:, tile * TILE : (tile + 1) * TILE, :]
                .reshape(2 * MODES_X * TILE, channels)
                .astype(low)
            )
        total_ref[...] = jnp.zeros_like(total_ref)

    coarse = coarse_ref[:, pl.ds(step, 1), :]
    summed = synthesise(
        rows,
        columns,
        channels,
        xfore_ref[...],
        yfore_ref,
        lambda tile: rowlow_ref[tile],
        lambda tile: colf_ref[:, tile * TILE : (tile + 1) * TILE, :],
        lambda place: coarse[place : place + 1],
    )
    count = rows * columns
    entering = summed.reshape(count, channels).astype(low)
    cotangent = cotangent_ref[...].reshape(count, channels)
    before = dot(entering, lift_ref[...])
    value, slope = gelu_pair(before)
    after_grad = dot(cotangent, dropt_ref[...])
    before_grad = (after_grad * slope).astype(low)
    total_ref[:, 0:hidden] += dot_tn(entering, before_grad)
    total_ref[:, hidden : 2 * hidden] += dot_tn(cotangent, value.astype(low))
    back = dot(before_grad, liftt_ref[...]).reshape(rows, columns, channels)
    analyse(back, step == 0, step, xback_ref, yback_ref, row_ref, column_ref, pool_ref)


def greet(sizes):
    barrier = pltpu.get_barrier_semaphore()
    count = 0
    for axis, size in sizes:
        me = lax.axis_index(axis)
        for k in range(1, size):
            pl.semaphore_signal(
                barrier, inc=1, device_id={axis: lax.rem(me + k, size)}, device_id_type=MESH
            )
            count += 1
    pl.semaphore_wait(barrier, count)


def send(axis, size, source_of, target_of, sems):
    me = lax.axis_index(axis)
    copies = []
    for k in range(1, size):
        dest = lax.rem(me + k, size)
        copy = pltpu.make_async_remote_copy(
            src_ref=source_of(dest),
            dst_ref=target_of(k - 1),
            send_sem=sems.at[0, k - 1],
            recv_sem=sems.at[1, k - 1],
            device_id={axis: dest},
            device_id_type=MESH,
        )
        copy.start()
        copies.append(copy)
    return copies


def arrive(copies):
    for copy in copies:
        copy.wait_recv()


def leave(copies):
    for copy in copies:
        copy.wait_send()


def sum_slots(own, slots_ref):
    for k in range(slots_ref.shape[0]):
        own = own + slots_ref[k]
    return own


def share(index, extent):
    return pl.ds(pl.multiple_of(index * extent, extent), extent)


def forward_kernel(
    n,
    m,
    scales,
    rowp_ref,
    colp_ref,
    poolp_ref,
    xweight_ref,
    yweight_ref,
    cweight_ref,
    mixrows_ref,
    rowown_ref,
    colown_ref,
    rowf_ref,
    colf_ref,
    pooled_ref,
    coarse_ref,
    rowslots,
    colslots,
    sem_row,
    sem_col,
    sem_pool,
    sem_rowf,
    sem_colf,
):
    scale_rows, scale_columns = scales
    px, py = lax.axis_index("gx"), lax.axis_index("gy")
    modes = MODES_X // n
    columns, channels = rowp_ref.shape[2:]
    rows = colp_ref.shape[2] // m
    width = poolp_ref.shape[0]
    greet((("gx", n), ("gy", m)))
    to_col = send(
        "gy", m, lambda d: colp_ref.at[:, :, share(d, rows)], lambda k: colslots.at[k], sem_col
    )
    to_row = send(
        "gx", n, lambda d: rowp_ref.at[:, share(d, modes)], lambda k: rowslots.at[k], sem_row
    )
    to_pool = send(
        "gy", m, lambda d: poolp_ref, lambda k: pooled_ref.at[share(py, width)], sem_pool
    )
    pooled_ref[share(py, width)] = poolp_ref[...]

    arrive(to_row)
    spec = sum_slots(rowp_ref[:, share(px, modes)], rowslots) * scale_rows
    rowown_ref[...] = spec
    for mode in range(modes):
        both = spec[:, mode].reshape(2 * columns, channels).astype(low)
        one = dot(both, xweight_ref[0, mode])
        two = dot(both, xweight_ref[1, mode])
        gain = 1.0 / math.sqrt(MODES_X)
        rowf_ref[0, px * modes + mode] = (one[:columns] - two[columns:]) * gain
        rowf_ref[1, px * modes + mode] = (two[:columns] + one[columns:]) * gain
    to_rowf = send(
        "gx",
        n,
        lambda d: rowf_ref.at[:, share(px, modes)],
        lambda k: rowf_ref.at[:, share(px, modes)],
        sem_rowf,
    )

    arrive(to_col)
    for mode in range(MODES_Y):
        spec = colp_ref[:, mode, share(py, rows)]
        for k in range(m - 1):
            spec = spec + colslots[k, :, mode]
        spec = spec * scale_columns
        colown_ref[:, mode] = spec
        both = spec.reshape(2 * rows, channels).astype(low)
        one = dot(both, yweight_ref[0, mode])
        two = dot(both, yweight_ref[1, mode])
        gain = 1.0 / math.sqrt(MODES_Y)
        colf_ref[0, mode, share(py, rows)] = (one[:rows] - two[rows:]) * gain
        colf_ref[1, mode, share(py, rows)] = (two[:rows] + one[rows:]) * gain
    to_colf = send(
        "gy",
        m,
        lambda d: colf_ref.at[:, :, share(py, rows)],
        lambda k: colf_ref.at[:, :, share(py, rows)],
        sem_colf,
    )

    arrive(to_pool)
    total_width, coarse_rows = pooled_ref.shape[:2]
    pooled = pooled_ref[...].reshape(total_width * coarse_rows, channels) * (1.0 / POOL)
    pre = dot(pooled.astype(low), cweight_ref[...])
    act, _ = gelu_pair(pre)
    coarse_ref[...] = dot(mixrows_ref[...], act.astype(low)).reshape(coarse_ref.shape)

    arrive(to_rowf)
    arrive(to_colf)
    for copies in (to_row, to_col, to_pool, to_rowf, to_colf):
        leave(copies)


def backward_kernel(
    n,
    m,
    scales,
    cotangent_ref,
    rowp_ref,
    colp_ref,
    poolp_ref,
    total_ref,
    rowown_ref,
    colown_ref,
    pooled_ref,
    xweight_ref,
    yweight_ref,
    cweight_ref,
    mixback_ref,
    xfore_ref,
    yfore_ref,
    cell_ref,
    totalf_ref,
    xgrad_ref,
    ygrad_ref,
    cgrad_ref,
    rowslots,
    colslots,
    rowf_ref,
    colf_ref,
    grads_ref,
    pregrad_ref,
    poolgrad_ref,
    totalslots,
    totalall,
    xpart,
    xslots,
    ypart,
    yslots,
    ychunk,
    ycslots,
    cpart,
    cslots,
    rowlow_ref,
    sem_row,
    sem_col,
    sem_pool,
    sem_rowf,
    sem_colf,
    sem_t,
    sem_tg,
    sem_tf,
    sem_x,
    sem_xf,
    sem_y,
    sem_yc,
    sem_ycf,
    sem_yf,
    sem_c,
    sem_cf,
):
    scale_rows, scale_columns = scales
    px, py = lax.axis_index("gx"), lax.axis_index("gy")
    modes = MODES_X // n
    columns, channels = rowp_ref.shape[2:]
    rows = colp_ref.shape[2] // m
    width, coarse_rows = poolp_ref.shape[:2]
    greet((("gx", n), ("gy", m)))
    to_pool = send(
        "gy", m, lambda d: poolp_ref, lambda k: grads_ref.at[share(py, width)], sem_pool
    )
    to_col = send(
        "gy", m, lambda d: colp_ref.at[:, :, share(d, rows)], lambda k: colslots.at[k], sem_col
    )
    to_row = send(
        "gx", n, lambda d: rowp_ref.at[:, share(d, modes)], lambda k: rowslots.at[k], sem_row
    )
    trows = total_ref.shape[0] // n
    to_t = send(
        "gx", n, lambda d: total_ref.at[share(d, trows)], lambda k: totalslots.at[k], sem_t
    )
    grads_ref[share(py, width)] = poolp_ref[...]

    arrive(to_pool)
    total_width = grads_ref.shape[0]
    count = total_width * coarse_rows
    pooled = (pooled_ref[...].reshape(count, channels) * (1.0 / POOL)).astype(low)
    pre = dot(pooled, cweight_ref[...])
    act, slope = gelu_pair(pre)
    grads = grads_ref[...].reshape(count, channels).astype(low)
    pre_grad = dot(mixback_ref[...], grads) * slope
    pregrad_ref[...] = pre_grad.reshape(pregrad_ref.shape)
    cpart[:, 0:channels] = dot_tn(pooled, pre_grad.astype(low))
    cross = dot_nt(grads, act.astype(low))
    left = lax.broadcasted_iota(jnp.int32, (count, count), 0) % coarse_rows
    right = lax.broadcasted_iota(jnp.int32, (count, count), 1) % coarse_rows
    cross = jnp.where(left == right, cross, 0.0)
    pick = (
        lax.broadcasted_iota(jnp.int32, (channels, count), 0)
        == lax.broadcasted_iota(jnp.int32, (channels, count), 1) // coarse_rows
    ).astype(wide)
    highest = lax.Precision.HIGHEST
    half = jnp.dot(pick, cross, precision=highest, preferred_element_type=wide)
    cpart[:, channels : 2 * channels] = lax.dot_general(
        half, pick, (((1,), (1,)), ((), ())), precision=highest, preferred_element_type=wide
    )
    crows = cpart.shape[0] // n
    to_c = send("gx", n, lambda d: cpart.at[share(d, crows)], lambda k: cslots.at[k], sem_c)
    own_grad = pregrad_ref[share(py, width)].reshape(width * coarse_rows, channels)
    poolgrad_ref[...] = (dot_nt(own_grad.astype(low), cweight_ref[...]) * (1.0 / POOL)).reshape(
        poolgrad_ref.shape
    )

    def mix_back(spec, grad, real_weight, imaginary_weight):
        half_rows = spec.shape[0] // 2
        grad_low = grad.astype(low)
        turned = jnp.concatenate([grad[half_rows:], -grad[:half_rows]], axis=0).astype(low)
        spec_low = spec.astype(low)
        back = dot_nt(grad_low, real_weight) + dot_nt(turned, imaginary_weight)
        return dot_tn(spec_low, grad_low), dot_tn(spec_low, turned), back

    arrive(to_row)
    grad = sum_slots(rowp_ref[:, share(px, modes)], rowslots) * (1.0 / math.sqrt(MODES_X))
    for mode in range(modes):
        real, imaginary, back = mix_back(
            rowown_ref[:, mode].reshape(2 * columns, channels),
            grad[:, mode].reshape(2 * columns, channels),
            xweight_ref[0, mode],
            xweight_ref[1, mode],
        )
        xpart[pl.ds(mode * channels, channels)] = real
        xpart[pl.ds((modes + mode) * channels, channels)] = imaginary
        rowf_ref[0, px * modes + mode] = back[:columns] * scale_rows
        rowf_ref[1, px * modes + mode] = back[columns:] * scale_rows
    to_rowf = send(
        "gx",
        n,
        lambda d: rowf_ref.at[:, share(px, modes)],
        lambda k: rowf_ref.at[:, share(px, modes)],
        sem_rowf,
    )

    arrive(to_col)
    for mode in range(MODES_Y):
        grad = colp_ref[:, mode, share(py, rows)]
        for k in range(m - 1):
            grad = grad + colslots[k, :, mode]
        grad = grad * (1.0 / math.sqrt(MODES_Y))
        real, imaginary, back = mix_back(
            colown_ref[:, mode].reshape(2 * rows, channels),
            grad.reshape(2 * rows, channels),
            yweight_ref[0, mode],
            yweight_ref[1, mode],
        )
        ypart[pl.ds(mode * channels, channels)] = real
        ypart[pl.ds((MODES_Y + mode) * channels, channels)] = imaginary
        colf_ref[0, mode, share(py, rows)] = back[:rows] * scale_columns
        colf_ref[1, mode, share(py, rows)] = back[rows:] * scale_columns
    to_colf = send(
        "gy",
        m,
        lambda d: colf_ref.at[:, :, share(py, rows)],
        lambda k: colf_ref.at[:, :, share(py, rows)],
        sem_colf,
    )
    yrows = ypart.shape[0] // n
    to_y = send("gx", n, lambda d: ypart.at[share(d, yrows)], lambda k: yslots.at[k], sem_y)
    xrows = xpart.shape[0] // m
    to_x = send("gy", m, lambda d: xpart.at[share(d, xrows)], lambda k: xslots.at[k], sem_x)

    arrive(to_t)
    totalall[py] = sum_slots(total_ref[share(px, trows)], totalslots)
    to_tg = send("gy", m, lambda d: totalall.at[py], lambda k: totalall.at[py], sem_tg)
    arrive(to_c)
    cgrad_ref[share(px, crows)] = sum_slots(cpart[share(px, crows)], cslots)
    to_cf = send(
        "gx",
        n,
        lambda d: cgrad_ref.at[share(px, crows)],
        lambda k: cgrad_ref.at[share(px, crows)],
        sem_cf,
    )

    block = POOL

    def field(step):
        xfore = xfore_ref[pl.ds(pl.multiple_of(step * (block * TILE), block * TILE), block * TILE)]
        coarse = poolgrad_ref[:, pl.ds(step, 1), :]

        def column_of(tile):
            begin = pl.multiple_of(step * block + tile * TILE, TILE)
            return colf_ref[:, :, pl.ds(begin, TILE), :]

        got = synthesise(
            block,
            columns,
            channels,
            xfore,
            yfore_ref,
            lambda tile: rowlow_ref[tile],
            column_of,
            lambda place: coarse[place : place + 1],
        )
        own = pl.ds(pl.multiple_of(step * block, block), block)
        cell_ref[own] = (cotangent_ref[own].astype(wide) + got).astype(low)

    arrive(to_rowf)
    for tile in range(columns // TILE):
        rowlow_ref[tile] = (
            rowf_ref[:, :, tile * TILE : (tile + 1) * TILE, :]
            .reshape(2 * MODES_X * TILE, channels)
            .astype(low)
        )
    arrive(to_y)
    ychunk[...] = sum_slots(ypart[share(px, yrows)], yslots)
    ycrows = yrows // m
    to_yc = send("gy", m, lambda d: ychunk.at[share(d, ycrows)], lambda k: ycslots.at[k], sem_yc)
    arrive(to_x)
    xgrad_ref[share(py, xrows)] = sum_slots(xpart[share(py, xrows)], xslots)
    to_xf = send(
        "gy",
        m,
        lambda d: xgrad_ref.at[share(py, xrows)],
        lambda k: xgrad_ref.at[share(py, xrows)],
        sem_xf,
    )
    arrive(to_tg)
    whole_total = totalall[0]
    for k in range(1, m):
        whole_total = whole_total + totalall[k]
    totalf_ref[share(px, trows)] = whole_total
    to_tf = send(
        "gx",
        n,
        lambda d: totalf_ref.at[share(px, trows)],
        lambda k: totalf_ref.at[share(px, trows)],
        sem_tf,
    )
    arrive(to_colf)
    steps = cell_ref.shape[0] // block
    early = steps // 2

    @pl.loop(0, early)
    def _(step):
        field(step)

    arrive(to_yc)
    own_y = pl.ds(pl.multiple_of(px * yrows + py * ycrows, ycrows), ycrows)
    ygrad_ref[own_y] = sum_slots(ychunk[share(py, ycrows)], ycslots)
    to_ycf = send("gy", m, lambda d: ygrad_ref.at[own_y], lambda k: ygrad_ref.at[own_y], sem_ycf)
    arrive(to_ycf)
    to_yf = send(
        "gx",
        n,
        lambda d: ygrad_ref.at[share(px, yrows)],
        lambda k: ygrad_ref.at[share(px, yrows)],
        sem_yf,
    )

    @pl.loop(early, steps)
    def _(step):
        field(step)

    for copies in (to_cf, to_xf, to_tf, to_yf):
        arrive(copies)
    for copies in (
        to_pool,
        to_col,
        to_row,
        to_t,
        to_c,
        to_rowf,
        to_colf,
        to_y,
        to_x,
        to_tg,
        to_cf,
        to_yc,
        to_xf,
        to_tf,
        to_ycf,
        to_yf,
    ):
        leave(copies)


def spread(rows, columns, row_of, column_of, table, keep):
    left = (
        row_of(lax.broadcasted_iota(jnp.int32, (rows, table.shape[0]), 0))
        == lax.broadcasted_iota(jnp.int32, (rows, table.shape[0]), 1)
    ).astype(low)
    right = (
        column_of(lax.broadcasted_iota(jnp.int32, (table.shape[1], columns), 1))
        == lax.broadcasted_iota(jnp.int32, (table.shape[1], columns), 0)
    ).astype(low)
    full = dot(dot(left, table).astype(low), right)
    place_row = lax.broadcasted_iota(jnp.int32, (rows, columns), 0)
    place_column = lax.broadcasted_iota(jnp.int32, (rows, columns), 1)
    return jnp.where(keep(place_row, place_column), full, 0.0).astype(low)


def remote(size):
    return pltpu.SemaphoreType.DMA((2, size - 1))


def on_device(
    n,
    m,
    cells,
    cotangent,
    lift_weight,
    drop_weight,
    xmode_weight,
    ymode_weight,
    coarse_weight,
    coarse_mix,
):
    rows, columns, channels = cells.shape
    hidden = lift_weight.shape[1]
    row_total, column_total = rows * n, columns * m
    coarse_rows, width = rows // POOL, columns // POOL
    total_width = width * m
    modes = MODES_X // n
    row_share = rows // m
    px, py = lax.axis_index("gx"), lax.axis_index("gy")
    row_basis = lax.dynamic_slice_in_dim(
        jnp.asarray(basis_table(MODES_X, row_total)), px * rows, rows, 1
    ).astype(low)
    column_basis = lax.dynamic_slice_in_dim(
        jnp.asarray(basis_table(MODES_Y, column_total)), py * columns, columns, 1
    ).astype(low)
    by_tile = lambda v: v // TILE
    same_tile = lambda r, c: r % TILE == c % TILE
    xfore = spread(rows * TILE, 2 * MODES_X * TILE, by_tile, by_tile, row_basis.T, same_tile)
    xback = spread(2 * MODES_X * TILE, rows * TILE, by_tile, by_tile, row_basis, same_tile)
    in_columns = lambda v: v % columns
    yfore = spread(
        TILE * columns,
        2 * MODES_Y * TILE,
        in_columns,
        by_tile,
        column_basis.T,
        lambda r, c: r // columns == c % TILE,
    )
    yback = spread(
        2 * MODES_Y * TILE,
        TILE * columns,
        by_tile,
        in_columns,
        column_basis,
        lambda r, c: r % TILE == c // columns,
    )
    by_coarse = lambda v: v // coarse_rows
    same_coarse = lambda r, c: r % coarse_rows == c % coarse_rows
    mix_rows = lax.dynamic_slice_in_dim(coarse_mix, py * width, width, 0)
    mix_fore = spread(
        width * coarse_rows, total_width * coarse_rows, by_coarse, by_coarse, mix_rows, same_coarse
    )
    mix_back = spread(
        total_width * coarse_rows,
        total_width * coarse_rows,
        by_coarse,
        by_coarse,
        coarse_mix.T,
        same_coarse,
    )
    steps = rows // POOL
    block_spec = pl.BlockSpec((POOL, columns, channels), lambda i: (i, 0, 0))

    def whole(*shape):
        return pl.BlockSpec(shape, lambda i: (0,) * len(shape))

    xback_spec = pl.BlockSpec((2 * MODES_X * TILE, POOL * TILE), lambda i: (0, i))
    xfore_spec = pl.BlockSpec((POOL * TILE, 2 * MODES_X * TILE), lambda i: (i, 0))
    column_spec = pl.BlockSpec((2 * MODES_Y, POOL, channels), lambda i: (0, i, 0))
    analysis_out = [
        jax.ShapeDtypeStruct((2 * MODES_X, columns, channels), wide),
        jax.ShapeDtypeStruct((2 * MODES_Y, rows, channels), wide),
        jax.ShapeDtypeStruct((width, coarse_rows, channels), wide),
    ]
    analysis_specs = [
        whole(2 * MODES_X, columns, channels),
        column_spec,
        whole(width, coarse_rows, channels),
    ]
    sequential = pltpu.CompilerParams(dimension_semantics=("arbitrary",))
    row_part, column_part, pool_part = pl.pallas_call(
        analysis_kernel,
        grid=(steps,),
        in_specs=[block_spec, xback_spec, whole(*yback.shape)],
        out_specs=analysis_specs,
        out_shape=analysis_out,
        compiler_params=sequential,
        name="analysis",
    )(cells, xback, yback)

    scales = (1.0 / math.sqrt(row_total), 1.0 / math.sqrt(column_total))
    row_shape = (2, MODES_X, columns, channels)
    column_shape = (2, MODES_Y, rows, channels)
    f32 = lambda *shape: jax.ShapeDtypeStruct(shape, wide)
    vm = lambda *shape: pltpu.VMEM(shape, wide)
    row_own, column_own, row_full, column_full, pooled, coarse_own = pl.pallas_call(
        functools.partial(forward_kernel, n, m, scales),
        out_shape=[
            f32(2, modes, columns, channels),
            f32(2, MODES_Y, row_share, channels),
            f32(*row_shape),
            f32(*column_shape),
            f32(total_width, coarse_rows, channels),
            f32(width, coarse_rows, channels),
        ],
        in_specs=[VMEM_SPEC] * 7,
        out_specs=[VMEM_SPEC] * 6,
        scratch_shapes=[
            vm(n - 1, 2, modes, columns, channels),
            vm(m - 1, 2, MODES_Y, row_share, channels),
            remote(n),
            remote(m),
            remote(m),
            remote(n),
            remote(m),
        ],
        compiler_params=pltpu.CompilerParams(collective_id=0, has_side_effects=True),
        name="forward_exchange",
    )(
        row_part.reshape(row_shape),
        column_part.reshape(column_shape),
        pool_part,
        xmode_weight,
        ymode_weight,
        coarse_weight,
        mix_fore,
    )

    row_back, column_back, pool_back, totals = pl.pallas_call(
        ffn_kernel,
        grid=(steps,),
        in_specs=[
            block_spec,
            whole(2 * MODES_X, columns, channels),
            column_spec,
            whole(width, coarse_rows, channels),
            whole(channels, hidden),
            whole(hidden, channels),
            whole(channels, hidden),
            xfore_spec,
            xback_spec,
            whole(*yfore.shape),
            whole(*yback.shape),
        ],
        out_specs=analysis_specs + [whole(channels, 2 * hidden)],
        out_shape=analysis_out + [f32(channels, 2 * hidden)],
        scratch_shapes=[pltpu.VMEM((columns // TILE, 2 * MODES_X * TILE, channels), low)],
        compiler_params=sequential,
        name="feed_forward",
    )(
        cotangent,
        row_full.reshape(2 * MODES_X, columns, channels),
        column_full.reshape(2 * MODES_Y, rows, channels),
        coarse_own,
        lift_weight,
        lift_weight.T,
        drop_weight.T,
        xfore,
        xback,
        yfore,
        yback,
    )

    trows = channels // n
    xrows = 2 * modes * channels
    yrows = 2 * MODES_Y * channels
    cell_grad, total_full, x_grad, y_grad, c_grad = pl.pallas_call(
        functools.partial(backward_kernel, n, m, scales),
        out_shape=[
            jax.ShapeDtypeStruct(cells.shape, low),
            f32(channels, 2 * hidden),
            f32(xrows, channels),
            f32(yrows, channels),
            f32(channels, 2 * channels),
        ],
        in_specs=[VMEM_SPEC] * 14,
        out_specs=[VMEM_SPEC] * 5,
        scratch_shapes=[
            vm(n - 1, 2, modes, columns, channels),
            vm(m - 1, 2, MODES_Y, row_share, channels),
            vm(*row_shape),
            vm(*column_shape),
            vm(total_width, coarse_rows, channels),
            vm(total_width, coarse_rows, channels),
            vm(width, coarse_rows, channels),
            vm(n - 1, trows, 2 * hidden),
            vm(m, trows, 2 * hidden),
            vm(xrows, channels),
            vm(m - 1, xrows // m, channels),
            vm(yrows, channels),
            vm(n - 1, yrows // n, channels),
            vm(yrows // n, channels),
            vm(m - 1, yrows // n // m, channels),
            vm(channels, 2 * channels),
            vm(n - 1, trows, 2 * channels),
            pltpu.VMEM((columns // TILE, 2 * MODES_X * TILE, channels), low),
            remote(n),
            remote(m),
            remote(m),
            remote(n),
            remote(m),
            remote(n),
            remote(m),
            remote(n),
            remote(m),
            remote(m),
            remote(n),
            remote(m),
            remote(m),
            remote(n),
            remote(n),
            remote(n),
        ],
        compiler_params=pltpu.CompilerParams(collective_id=1, has_side_effects=True),
        name="backward_exchange",
    )(
        cotangent,
        row_back.reshape(row_shape),
        column_back.reshape(column_shape),
        pool_back,
        totals,
        row_own,
        column_own,
        pooled,
        xmode_weight,
        ymode_weight,
        coarse_weight,
        mix_back,
        xfore,
        yfore,
    )
    return (
        cell_grad,
        total_full[:, :hidden],
        total_full[:, hidden:].T,
        x_grad.reshape(2, modes, channels, channels),
        y_grad.reshape(2, MODES_Y, channels, channels),
        c_grad[:, :channels],
        c_grad[:total_width, channels : channels + total_width],
    )


def solution(mesh):
    in_specs = (
        P("gx", "gy", None),
        P("gx", "gy", None),
        P(),
        P(),
        P(None, "gx", None, None),
        P(),
        P(),
        P(),
    )
    out_specs = (P("gx", "gy", None), P(), P(), P(None, "gx", None, None), P(), P(), P())
    return jax.shard_map(
        functools.partial(on_device, mesh.shape["gx"], mesh.shape["gy"]),
        mesh=mesh,
        in_specs=in_specs,
        out_specs=out_specs,
        check_vma=False,
    )
```

```python
import functools
import math

import jax
import jax.numpy as jnp
import numpy as np
from jax import lax
from jax.experimental import pallas as pl
from jax.experimental.pallas import tpu as pltpu
from jax.sharding import PartitionSpec as P

MODES_X = 16
MODES_Y = 8
POOL = 16
TILE = 8

gelu_scale = 0.7978845608028654
gelu_cubic = 0.044715
MESH = pl.DeviceIdType.MESH
VMEM_SPEC = pl.BlockSpec(memory_space=pltpu.VMEM)
low = jnp.bfloat16
wide = jnp.float32


def gelu_pair(values):
    square = values * values
    tangent = jnp.tanh(values * (gelu_scale + (gelu_scale * gelu_cubic) * square))
    half = 0.5 + 0.5 * tangent
    bend = values * (0.5 * gelu_scale + (1.5 * gelu_scale * gelu_cubic) * square)
    return values * half, half + bend * (1.0 - tangent * tangent)


def dot(former, latter):
    return jnp.dot(former, latter, preferred_element_type=wide)


def dot_nt(former, latter):
    return lax.dot_general(former, latter, (((1,), (1,)), ((), ())), preferred_element_type=wide)


def dot_tn(former, latter):
    return lax.dot_general(former, latter, (((0,), (0,)), ((), ())), preferred_element_type=wide)


def halves(values):
    high = values.astype(low)
    return high, (values - high.astype(wide)).astype(low)


def dot_fine(former, latter):
    return sum(dot(part, latter) for part in halves(former))


def dot_nt_fine(former, latter):
    return sum(dot_nt(part, latter) for part in halves(former))


def dot_tn_fine(former, latter):
    high, rest = halves(former)
    other, other_rest = halves(latter)
    return dot_tn(high, other) + dot_tn(high, other_rest) + dot_tn(rest, other)


def basis_table(mode_count, length):
    phase = np.outer(np.arange(mode_count), np.arange(length)) % length
    angles = phase * (2.0 * math.pi / length)
    return np.concatenate([np.cos(angles), -np.sin(angles)], axis=0).astype(np.float32)


def analyse(block, first, step, xback_ref, yback_ref, row_ref, column_ref, pool_ref):
    rows, columns, channels = block.shape
    for pair in range(columns // TILE // 2):
        sides = []
        for tile in (2 * pair, 2 * pair + 1):
            piece = block[:, tile * TILE : (tile + 1) * TILE, :]
            sides.append(piece.reshape(rows * TILE, channels).astype(low))
        part = dot(xback_ref[...], jnp.concatenate(sides, axis=1))
        for side in range(2):
            own = pl.ds((2 * pair + side) * TILE, TILE)
            mine = part[:, side * channels : (side + 1) * channels]
            mine = mine.reshape(2 * MODES_X, TILE, channels)

            @pl.when(first)
            def _():
                row_ref[:, own, :] = mine

            @pl.when(jnp.logical_not(first))
            def _():
                row_ref[:, own, :] += mine

    for pair in range(rows // TILE // 2):
        sides = []
        for tile in (2 * pair, 2 * pair + 1):
            piece = block[tile * TILE : (tile + 1) * TILE].reshape(TILE * columns, channels)
            sides.append(piece.astype(low))
        part = dot(yback_ref[...], jnp.concatenate(sides, axis=1))
        for side in range(2):
            own = pl.ds((2 * pair + side) * TILE, TILE)
            mine = part[:, side * channels : (side + 1) * channels]
            column_ref[:, own, :] = mine.reshape(2 * MODES_Y, TILE, channels)
    pooled = block.sum(axis=0).reshape(columns // POOL, POOL, channels).sum(axis=1)
    pool_ref[:, pl.ds(step, 1), :] = pooled[:, None, :]


def analysis_kernel(cells_ref, xback_ref, yback_ref, row_ref, column_ref, pool_ref):
    step = pl.program_id(0)
    block = cells_ref[...].astype(wide)
    analyse(block, step == 0, step, xback_ref, yback_ref, row_ref, column_ref, pool_ref)


def synthesise(rows, columns, channels, xfore, yfore_ref, row_low, column_of, coarse_of):
    parts = []
    for pair in range(rows // TILE // 2):
        sides = []
        for tile in (2 * pair, 2 * pair + 1):
            modes = column_of(tile).reshape(2 * MODES_Y * TILE, channels)
            sides.append(modes.astype(low))
        both = dot(yfore_ref[...], jnp.concatenate(sides, axis=1))
        for side in range(2):
            mine = both[:, side * channels : (side + 1) * channels]
            parts.append(mine.reshape(TILE, columns, channels))
    field = jnp.concatenate(parts, axis=0)
    pieces = []
    for pair in range(columns // TILE // 2):
        both = dot(xfore, row_low(pair))
        for side in range(2):
            mine = both[:, side * channels : (side + 1) * channels]
            part = mine.reshape(rows, TILE, channels)
            pieces.append(part + coarse_of((2 * pair + side) * TILE // POOL))
    return field + jnp.concatenate(pieces, axis=1)


def fill_low(low_ref, tile_of, columns, channels):
    for tile in range(columns // TILE):
        lanes = slice(tile % 2 * channels, (tile % 2 + 1) * channels)
        modes = tile_of(tile).reshape(2 * MODES_X * TILE, channels)
        low_ref[tile // 2, :, lanes] = modes.astype(low)


def ffn_kernel(
    cotangent_ref,
    rowf_ref,
    colf_ref,
    coarse_ref,
    lift_ref,
    liftt_ref,
    dropt_ref,
    xfore_ref,
    xback_ref,
    yfore_ref,
    yback_ref,
    row_ref,
    column_ref,
    pool_ref,
    total_ref,
    rowlow_ref,
):
    step = pl.program_id(0)
    rows, columns, channels = cotangent_ref.shape
    hidden = lift_ref.shape[1]

    @pl.when(step == 0)
    def _():
        fill_low(
            rowlow_ref,
            lambda tile: rowf_ref[:, tile * TILE : (tile + 1) * TILE, :],
            columns,
            channels,
        )
        total_ref[...] = jnp.zeros_like(total_ref)

    coarse = coarse_ref[:, pl.ds(step, 1), :]
    summed = synthesise(
        rows,
        columns,
        channels,
        xfore_ref[...],
        yfore_ref,
        lambda pair: rowlow_ref[pair],
        lambda tile: colf_ref[:, tile * TILE : (tile + 1) * TILE, :],
        lambda place: coarse[place : place + 1],
    )
    count = rows * columns
    entering = summed.reshape(count, channels).astype(low)
    cotangent = cotangent_ref[...].reshape(count, channels)
    before = dot(entering, lift_ref[...])
    value, slope = gelu_pair(before)
    after_grad = dot(cotangent, dropt_ref[...])
    before_grad = (after_grad * slope).astype(low)
    total_ref[:, 0:hidden] += dot_tn(entering, before_grad)
    total_ref[:, hidden : 2 * hidden] += dot_tn(cotangent, value.astype(low))
    back = dot(before_grad, liftt_ref[...]).reshape(rows, columns, channels)
    analyse(back, step == 0, step, xback_ref, yback_ref, row_ref, column_ref, pool_ref)


def greet(sizes):
    barrier = pltpu.get_barrier_semaphore()
    count = 0
    for axis, size in sizes:
        me = lax.axis_index(axis)
        for k in range(1, size):
            pl.semaphore_signal(
                barrier, inc=1, device_id={axis: lax.rem(me + k, size)}, device_id_type=MESH
            )
            count += 1
    pl.semaphore_wait(barrier, count)


def send(axis, size, source_of, target_of, sems):
    me = lax.axis_index(axis)
    copies = []
    for k in range(1, size):
        dest = lax.rem(me + k, size)
        copy = pltpu.make_async_remote_copy(
            src_ref=source_of(dest),
            dst_ref=target_of(k - 1),
            send_sem=sems.at[0, k - 1],
            recv_sem=sems.at[1, k - 1],
            device_id={axis: dest},
            device_id_type=MESH,
        )
        copy.start()
        copies.append(copy)
    return copies


def arrive(copies):
    for copy in copies:
        copy.wait_recv()


def leave(copies):
    for copy in copies:
        copy.wait_send()


def sum_slots(own, slots_ref):
    for k in range(slots_ref.shape[0]):
        own = own + slots_ref[k]
    return own


def share(index, extent):
    return pl.ds(pl.multiple_of(index * extent, extent), extent)


def forward_kernel(
    n,
    m,
    scales,
    rowp_ref,
    colp_ref,
    poolp_ref,
    xweight_ref,
    yweight_ref,
    cweight_ref,
    mixrows_ref,
    rowown_ref,
    colown_ref,
    rowf_ref,
    colf_ref,
    pooled_ref,
    coarse_ref,
    rowslots,
    colslots,
    sem_row,
    sem_col,
    sem_pool,
    sem_rowf,
    sem_colf,
):
    scale_rows, scale_columns = scales
    px, py = lax.axis_index("gx"), lax.axis_index("gy")
    modes = MODES_X // n
    columns, channels = rowp_ref.shape[2:]
    rows = colp_ref.shape[2] // m
    width = poolp_ref.shape[0]
    greet((("gx", n), ("gy", m)))
    to_col = send(
        "gy", m, lambda d: colp_ref.at[:, :, share(d, rows)], lambda k: colslots.at[k], sem_col
    )
    to_row = send(
        "gx", n, lambda d: rowp_ref.at[:, share(d, modes)], lambda k: rowslots.at[k], sem_row
    )
    to_pool = send(
        "gy", m, lambda d: poolp_ref, lambda k: pooled_ref.at[share(py, width)], sem_pool
    )
    pooled_ref[share(py, width)] = poolp_ref[...]

    arrive(to_row)
    spec = sum_slots(rowp_ref[:, share(px, modes)], rowslots) * scale_rows
    rowown_ref[...] = spec
    for mode in range(modes):
        both = spec[:, mode].reshape(2 * columns, channels)
        one = dot_fine(both, xweight_ref[0, mode])
        two = dot_fine(both, xweight_ref[1, mode])
        gain = 1.0 / math.sqrt(MODES_X)
        rowf_ref[0, px * modes + mode] = (one[:columns] - two[columns:]) * gain
        rowf_ref[1, px * modes + mode] = (two[:columns] + one[columns:]) * gain
    to_rowf = send(
        "gx",
        n,
        lambda d: rowf_ref.at[:, share(px, modes)],
        lambda k: rowf_ref.at[:, share(px, modes)],
        sem_rowf,
    )

    arrive(to_col)
    for mode in range(MODES_Y):
        spec = colp_ref[:, mode, share(py, rows)]
        for k in range(m - 1):
            spec = spec + colslots[k, :, mode]
        spec = spec * scale_columns
        colown_ref[:, mode] = spec
        both = spec.reshape(2 * rows, channels)
        one = dot_fine(both, yweight_ref[0, mode])
        two = dot_fine(both, yweight_ref[1, mode])
        gain = 1.0 / math.sqrt(MODES_Y)
        colf_ref[0, mode, share(py, rows)] = (one[:rows] - two[rows:]) * gain
        colf_ref[1, mode, share(py, rows)] = (two[:rows] + one[rows:]) * gain
    to_colf = send(
        "gy",
        m,
        lambda d: colf_ref.at[:, :, share(py, rows)],
        lambda k: colf_ref.at[:, :, share(py, rows)],
        sem_colf,
    )

    arrive(to_pool)
    total_width, coarse_rows = pooled_ref.shape[:2]
    pooled = pooled_ref[...].reshape(total_width * coarse_rows, channels) * (1.0 / POOL)
    pre = dot_fine(pooled, cweight_ref[...])
    act, _ = gelu_pair(pre)
    coarse_ref[...] = sum(dot(mixrows_ref[...], part) for part in halves(act)).reshape(coarse_ref.shape)

    arrive(to_rowf)
    arrive(to_colf)
    for copies in (to_row, to_col, to_pool, to_rowf, to_colf):
        leave(copies)


def backward_kernel(
    n,
    m,
    scales,
    cotangent_ref,
    rowp_ref,
    colp_ref,
    poolp_ref,
    total_ref,
    rowown_ref,
    colown_ref,
    pooled_ref,
    xweight_ref,
    yweight_ref,
    cweight_ref,
    mixback_ref,
    xfore_ref,
    yfore_ref,
    cell_ref,
    totalf_ref,
    xgrad_ref,
    ygrad_ref,
    cgrad_ref,
    rowslots,
    colslots,
    rowf_ref,
    colf_ref,
    grads_ref,
    pregrad_ref,
    poolgrad_ref,
    totalslots,
    totalall,
    xpart,
    xslots,
    ypart,
    yslots,
    ychunk,
    ycslots,
    cpart,
    cslots,
    rowlow_ref,
    sem_row,
    sem_col,
    sem_pool,
    sem_rowf,
    sem_colf,
    sem_t,
    sem_tg,
    sem_tf,
    sem_x,
    sem_xf,
    sem_y,
    sem_yc,
    sem_ycf,
    sem_yf,
    sem_c,
    sem_cf,
):
    scale_rows, scale_columns = scales
    px, py = lax.axis_index("gx"), lax.axis_index("gy")
    modes = MODES_X // n
    columns, channels = rowp_ref.shape[2:]
    rows = colp_ref.shape[2] // m
    width, coarse_rows = poolp_ref.shape[:2]
    greet((("gx", n), ("gy", m)))
    to_pool = send(
        "gy", m, lambda d: poolp_ref, lambda k: grads_ref.at[share(py, width)], sem_pool
    )
    to_col = send(
        "gy", m, lambda d: colp_ref.at[:, :, share(d, rows)], lambda k: colslots.at[k], sem_col
    )
    to_row = send(
        "gx", n, lambda d: rowp_ref.at[:, share(d, modes)], lambda k: rowslots.at[k], sem_row
    )
    trows = total_ref.shape[0] // n
    to_t = send(
        "gx", n, lambda d: total_ref.at[share(d, trows)], lambda k: totalslots.at[k], sem_t
    )
    grads_ref[share(py, width)] = poolp_ref[...]

    arrive(to_pool)
    total_width = grads_ref.shape[0]
    count = total_width * coarse_rows
    pooled = pooled_ref[...].reshape(count, channels) * (1.0 / POOL)
    pre = dot_fine(pooled, cweight_ref[...])
    act, slope = gelu_pair(pre)
    grads = grads_ref[...].reshape(count, channels).astype(low)
    pre_grad = dot(mixback_ref[...], grads) * slope
    pregrad_ref[...] = pre_grad.reshape(pregrad_ref.shape)
    cpart[:, 0:channels] = dot_tn_fine(pooled, pre_grad)
    cross = dot_nt(grads, act.astype(low))
    left = lax.broadcasted_iota(jnp.int32, (count, count), 0) % coarse_rows
    right = lax.broadcasted_iota(jnp.int32, (count, count), 1) % coarse_rows
    cross = jnp.where(left == right, cross, 0.0)
    pick = (
        lax.broadcasted_iota(jnp.int32, (channels, count), 0)
        == lax.broadcasted_iota(jnp.int32, (channels, count), 1) // coarse_rows
    ).astype(wide)
    highest = lax.Precision.HIGHEST
    half = jnp.dot(pick, cross, precision=highest, preferred_element_type=wide)
    cpart[:, channels : 2 * channels] = lax.dot_general(
        half, pick, (((1,), (1,)), ((), ())), precision=highest, preferred_element_type=wide
    )
    crows = cpart.shape[0] // n
    to_c = send("gx", n, lambda d: cpart.at[share(d, crows)], lambda k: cslots.at[k], sem_c)
    own_grad = pregrad_ref[share(py, width)].reshape(width * coarse_rows, channels)
    poolgrad_ref[...] = (dot_nt_fine(own_grad, cweight_ref[...]) * (1.0 / POOL)).reshape(
        poolgrad_ref.shape
    )

    def mix_back(spec, grad, real_weight, imaginary_weight):
        half_rows = spec.shape[0] // 2
        turned = jnp.concatenate([grad[half_rows:], -grad[:half_rows]], axis=0)
        back = dot_nt_fine(grad, real_weight) + dot_nt_fine(turned, imaginary_weight)
        return dot_tn_fine(spec, grad), dot_tn_fine(spec, turned), back

    arrive(to_row)
    grad = sum_slots(rowp_ref[:, share(px, modes)], rowslots) * (1.0 / math.sqrt(MODES_X))
    for mode in range(modes):
        real, imaginary, back = mix_back(
            rowown_ref[:, mode].reshape(2 * columns, channels),
            grad[:, mode].reshape(2 * columns, channels),
            xweight_ref[0, mode],
            xweight_ref[1, mode],
        )
        xpart[pl.ds(mode * channels, channels)] = real
        xpart[pl.ds((modes + mode) * channels, channels)] = imaginary
        rowf_ref[0, px * modes + mode] = back[:columns] * scale_rows
        rowf_ref[1, px * modes + mode] = back[columns:] * scale_rows
    to_rowf = send(
        "gx",
        n,
        lambda d: rowf_ref.at[:, share(px, modes)],
        lambda k: rowf_ref.at[:, share(px, modes)],
        sem_rowf,
    )

    arrive(to_col)
    for mode in range(MODES_Y):
        grad = colp_ref[:, mode, share(py, rows)]
        for k in range(m - 1):
            grad = grad + colslots[k, :, mode]
        grad = grad * (1.0 / math.sqrt(MODES_Y))
        real, imaginary, back = mix_back(
            colown_ref[:, mode].reshape(2 * rows, channels),
            grad.reshape(2 * rows, channels),
            yweight_ref[0, mode],
            yweight_ref[1, mode],
        )
        ypart[pl.ds(mode * channels, channels)] = real
        ypart[pl.ds((MODES_Y + mode) * channels, channels)] = imaginary
        colf_ref[0, mode, share(py, rows)] = back[:rows] * scale_columns
        colf_ref[1, mode, share(py, rows)] = back[rows:] * scale_columns
    to_colf = send(
        "gy",
        m,
        lambda d: colf_ref.at[:, :, share(py, rows)],
        lambda k: colf_ref.at[:, :, share(py, rows)],
        sem_colf,
    )
    yrows = ypart.shape[0] // n
    to_y = send("gx", n, lambda d: ypart.at[share(d, yrows)], lambda k: yslots.at[k], sem_y)
    xrows = xpart.shape[0] // m
    to_x = send("gy", m, lambda d: xpart.at[share(d, xrows)], lambda k: xslots.at[k], sem_x)

    arrive(to_t)
    totalall[py] = sum_slots(total_ref[share(px, trows)], totalslots)
    to_tg = send("gy", m, lambda d: totalall.at[py], lambda k: totalall.at[py], sem_tg)
    arrive(to_c)
    cgrad_ref[share(px, crows)] = sum_slots(cpart[share(px, crows)], cslots)
    to_cf = send(
        "gx",
        n,
        lambda d: cgrad_ref.at[share(px, crows)],
        lambda k: cgrad_ref.at[share(px, crows)],
        sem_cf,
    )

    block = POOL

    def field(step):
        xfore = xfore_ref[pl.ds(pl.multiple_of(step * (block * TILE), block * TILE), block * TILE)]
        coarse = poolgrad_ref[:, pl.ds(step, 1), :]

        def column_of(tile):
            begin = pl.multiple_of(step * block + tile * TILE, TILE)
            return colf_ref[:, :, pl.ds(begin, TILE), :]

        got = synthesise(
            block,
            columns,
            channels,
            xfore,
            yfore_ref,
            lambda pair: rowlow_ref[pair],
            column_of,
            lambda place: coarse[place : place + 1],
        )
        own = pl.ds(pl.multiple_of(step * block, block), block)
        cell_ref[own] = (cotangent_ref[own].astype(wide) + got).astype(low)

    arrive(to_rowf)
    fill_low(
        rowlow_ref,
        lambda tile: rowf_ref[:, :, tile * TILE : (tile + 1) * TILE, :],
        columns,
        channels,
    )
    arrive(to_y)
    ychunk[...] = sum_slots(ypart[share(px, yrows)], yslots)
    ycrows = yrows // m
    to_yc = send("gy", m, lambda d: ychunk.at[share(d, ycrows)], lambda k: ycslots.at[k], sem_yc)
    arrive(to_x)
    xgrad_ref[share(py, xrows)] = sum_slots(xpart[share(py, xrows)], xslots)
    to_xf = send(
        "gy",
        m,
        lambda d: xgrad_ref.at[share(py, xrows)],
        lambda k: xgrad_ref.at[share(py, xrows)],
        sem_xf,
    )
    arrive(to_tg)
    whole_total = totalall[0]
    for k in range(1, m):
        whole_total = whole_total + totalall[k]
    totalf_ref[share(px, trows)] = whole_total
    to_tf = send(
        "gx",
        n,
        lambda d: totalf_ref.at[share(px, trows)],
        lambda k: totalf_ref.at[share(px, trows)],
        sem_tf,
    )
    arrive(to_colf)
    steps = cell_ref.shape[0] // block
    early = steps // 2

    @pl.loop(0, early)
    def _(step):
        field(step)

    arrive(to_yc)
    own_y = pl.ds(pl.multiple_of(px * yrows + py * ycrows, ycrows), ycrows)
    ygrad_ref[own_y] = sum_slots(ychunk[share(py, ycrows)], ycslots)
    to_ycf = send("gy", m, lambda d: ygrad_ref.at[own_y], lambda k: ygrad_ref.at[own_y], sem_ycf)
    arrive(to_ycf)
    to_yf = send(
        "gx",
        n,
        lambda d: ygrad_ref.at[share(px, yrows)],
        lambda k: ygrad_ref.at[share(px, yrows)],
        sem_yf,
    )

    @pl.loop(early, steps)
    def _(step):
        field(step)

    for copies in (to_cf, to_xf, to_tf, to_yf):
        arrive(copies)
    for copies in (
        to_pool,
        to_col,
        to_row,
        to_t,
        to_c,
        to_rowf,
        to_colf,
        to_y,
        to_x,
        to_tg,
        to_cf,
        to_yc,
        to_xf,
        to_tf,
        to_ycf,
        to_yf,
    ):
        leave(copies)


def spread(rows, columns, row_of, column_of, table, keep):
    left = (
        row_of(lax.broadcasted_iota(jnp.int32, (rows, table.shape[0]), 0))
        == lax.broadcasted_iota(jnp.int32, (rows, table.shape[0]), 1)
    ).astype(low)
    right = (
        column_of(lax.broadcasted_iota(jnp.int32, (table.shape[1], columns), 1))
        == lax.broadcasted_iota(jnp.int32, (table.shape[1], columns), 0)
    ).astype(low)
    full = dot(dot(left, table).astype(low), right)
    place_row = lax.broadcasted_iota(jnp.int32, (rows, columns), 0)
    place_column = lax.broadcasted_iota(jnp.int32, (rows, columns), 1)
    return jnp.where(keep(place_row, place_column), full, 0.0).astype(low)


def remote(size):
    return pltpu.SemaphoreType.DMA((2, size - 1))


def on_device(
    n,
    m,
    cells,
    cotangent,
    lift_weight,
    drop_weight,
    xmode_weight,
    ymode_weight,
    coarse_weight,
    coarse_mix,
):
    rows, columns, channels = cells.shape
    hidden = lift_weight.shape[1]
    row_total, column_total = rows * n, columns * m
    coarse_rows, width = rows // POOL, columns // POOL
    total_width = width * m
    modes = MODES_X // n
    row_share = rows // m
    px, py = lax.axis_index("gx"), lax.axis_index("gy")
    row_basis = lax.dynamic_slice_in_dim(
        jnp.asarray(basis_table(MODES_X, row_total)), px * rows, rows, 1
    ).astype(low)
    column_basis = lax.dynamic_slice_in_dim(
        jnp.asarray(basis_table(MODES_Y, column_total)), py * columns, columns, 1
    ).astype(low)
    by_tile = lambda v: v // TILE
    same_tile = lambda r, c: r % TILE == c % TILE
    xfore = spread(rows * TILE, 2 * MODES_X * TILE, by_tile, by_tile, row_basis.T, same_tile)
    xback = spread(2 * MODES_X * TILE, rows * TILE, by_tile, by_tile, row_basis, same_tile)
    in_columns = lambda v: v % columns
    yfore = spread(
        TILE * columns,
        2 * MODES_Y * TILE,
        in_columns,
        by_tile,
        column_basis.T,
        lambda r, c: r // columns == c % TILE,
    )
    yback = spread(
        2 * MODES_Y * TILE,
        TILE * columns,
        by_tile,
        in_columns,
        column_basis,
        lambda r, c: r % TILE == c // columns,
    )
    by_coarse = lambda v: v // coarse_rows
    same_coarse = lambda r, c: r % coarse_rows == c % coarse_rows
    mix_rows = lax.dynamic_slice_in_dim(coarse_mix, py * width, width, 0)
    mix_fore = spread(
        width * coarse_rows, total_width * coarse_rows, by_coarse, by_coarse, mix_rows, same_coarse
    )
    mix_back = spread(
        total_width * coarse_rows,
        total_width * coarse_rows,
        by_coarse,
        by_coarse,
        coarse_mix.T,
        same_coarse,
    )
    steps = rows // POOL
    block_spec = pl.BlockSpec((POOL, columns, channels), lambda i: (i, 0, 0))

    def whole(*shape):
        return pl.BlockSpec(shape, lambda i: (0,) * len(shape))

    xback_spec = pl.BlockSpec((2 * MODES_X * TILE, POOL * TILE), lambda i: (0, i))
    xfore_spec = pl.BlockSpec((POOL * TILE, 2 * MODES_X * TILE), lambda i: (i, 0))
    column_spec = pl.BlockSpec((2 * MODES_Y, POOL, channels), lambda i: (0, i, 0))
    analysis_out = [
        jax.ShapeDtypeStruct((2 * MODES_X, columns, channels), wide),
        jax.ShapeDtypeStruct((2 * MODES_Y, rows, channels), wide),
        jax.ShapeDtypeStruct((width, coarse_rows, channels), wide),
    ]
    analysis_specs = [
        whole(2 * MODES_X, columns, channels),
        column_spec,
        whole(width, coarse_rows, channels),
    ]
    sequential = pltpu.CompilerParams(dimension_semantics=("arbitrary",))
    row_part, column_part, pool_part = pl.pallas_call(
        analysis_kernel,
        grid=(steps,),
        in_specs=[block_spec, xback_spec, whole(*yback.shape)],
        out_specs=analysis_specs,
        out_shape=analysis_out,
        compiler_params=sequential,
        name="analysis",
    )(cells, xback, yback)

    scales = (1.0 / math.sqrt(row_total), 1.0 / math.sqrt(column_total))
    row_shape = (2, MODES_X, columns, channels)
    column_shape = (2, MODES_Y, rows, channels)
    f32 = lambda *shape: jax.ShapeDtypeStruct(shape, wide)
    vm = lambda *shape: pltpu.VMEM(shape, wide)
    row_own, column_own, row_full, column_full, pooled, coarse_own = pl.pallas_call(
        functools.partial(forward_kernel, n, m, scales),
        out_shape=[
            f32(2, modes, columns, channels),
            f32(2, MODES_Y, row_share, channels),
            f32(*row_shape),
            f32(*column_shape),
            f32(total_width, coarse_rows, channels),
            f32(width, coarse_rows, channels),
        ],
        in_specs=[VMEM_SPEC] * 7,
        out_specs=[VMEM_SPEC] * 6,
        scratch_shapes=[
            vm(n - 1, 2, modes, columns, channels),
            vm(m - 1, 2, MODES_Y, row_share, channels),
            remote(n),
            remote(m),
            remote(m),
            remote(n),
            remote(m),
        ],
        compiler_params=pltpu.CompilerParams(collective_id=0, has_side_effects=True),
        name="forward_exchange",
    )(
        row_part.reshape(row_shape),
        column_part.reshape(column_shape),
        pool_part,
        xmode_weight,
        ymode_weight,
        coarse_weight,
        mix_fore,
    )

    row_back, column_back, pool_back, totals = pl.pallas_call(
        ffn_kernel,
        grid=(steps,),
        in_specs=[
            block_spec,
            whole(2 * MODES_X, columns, channels),
            column_spec,
            whole(width, coarse_rows, channels),
            whole(channels, hidden),
            whole(hidden, channels),
            whole(channels, hidden),
            xfore_spec,
            xback_spec,
            whole(*yfore.shape),
            whole(*yback.shape),
        ],
        out_specs=analysis_specs + [whole(channels, 2 * hidden)],
        out_shape=analysis_out + [f32(channels, 2 * hidden)],
        scratch_shapes=[pltpu.VMEM((columns // TILE // 2, 2 * MODES_X * TILE, 2 * channels), low)],
        compiler_params=sequential,
        name="feed_forward",
    )(
        cotangent,
        row_full.reshape(2 * MODES_X, columns, channels),
        column_full.reshape(2 * MODES_Y, rows, channels),
        coarse_own,
        lift_weight,
        lift_weight.T,
        drop_weight.T,
        xfore,
        xback,
        yfore,
        yback,
    )

    trows = channels // n
    xrows = 2 * modes * channels
    yrows = 2 * MODES_Y * channels
    cell_grad, total_full, x_grad, y_grad, c_grad = pl.pallas_call(
        functools.partial(backward_kernel, n, m, scales),
        out_shape=[
            jax.ShapeDtypeStruct(cells.shape, low),
            f32(channels, 2 * hidden),
            f32(xrows, channels),
            f32(yrows, channels),
            f32(channels, 2 * channels),
        ],
        in_specs=[VMEM_SPEC] * 14,
        out_specs=[VMEM_SPEC] * 5,
        scratch_shapes=[
            vm(n - 1, 2, modes, columns, channels),
            vm(m - 1, 2, MODES_Y, row_share, channels),
            vm(*row_shape),
            vm(*column_shape),
            vm(total_width, coarse_rows, channels),
            vm(total_width, coarse_rows, channels),
            vm(width, coarse_rows, channels),
            vm(n - 1, trows, 2 * hidden),
            vm(m, trows, 2 * hidden),
            vm(xrows, channels),
            vm(m - 1, xrows // m, channels),
            vm(yrows, channels),
            vm(n - 1, yrows // n, channels),
            vm(yrows // n, channels),
            vm(m - 1, yrows // n // m, channels),
            vm(channels, 2 * channels),
            vm(n - 1, trows, 2 * channels),
            pltpu.VMEM((columns // TILE // 2, 2 * MODES_X * TILE, 2 * channels), low),
            remote(n),
            remote(m),
            remote(m),
            remote(n),
            remote(m),
            remote(n),
            remote(m),
            remote(n),
            remote(m),
            remote(m),
            remote(n),
            remote(m),
            remote(m),
            remote(n),
            remote(n),
            remote(n),
        ],
        compiler_params=pltpu.CompilerParams(collective_id=1, has_side_effects=True),
        name="backward_exchange",
    )(
        cotangent,
        row_back.reshape(row_shape),
        column_back.reshape(column_shape),
        pool_back,
        totals,
        row_own,
        column_own,
        pooled,
        xmode_weight,
        ymode_weight,
        coarse_weight,
        mix_back,
        xfore,
        yfore,
    )
    return (
        cell_grad,
        total_full[:, :hidden],
        total_full[:, hidden:].T,
        x_grad.reshape(2, modes, channels, channels),
        y_grad.reshape(2, MODES_Y, channels, channels),
        c_grad[:, :channels],
        c_grad[:total_width, channels : channels + total_width],
    )


def solution(mesh):
    in_specs = (
        P("gx", "gy", None),
        P("gx", "gy", None),
        P(),
        P(),
        P(None, "gx", None, None),
        P(),
        P(),
        P(),
    )
    out_specs = (P("gx", "gy", None), P(), P(), P(None, "gx", None, None), P(), P(), P())
    return jax.shard_map(
        functools.partial(on_device, mesh.shape["gx"], mesh.shape["gy"]),
        mesh=mesh,
        in_specs=in_specs,
        out_specs=out_specs,
        check_vma=False,
    )
```

```python
import functools
import math

import jax
import jax.numpy as jnp
import numpy as np
from jax import lax
from jax.experimental import pallas as pl
from jax.experimental.pallas import tpu as pltpu
from jax.sharding import PartitionSpec as P

MODES_X = 16
MODES_Y = 8
POOL = 16
TILE = 8
PIECES = 4

gelu_scale = 0.7978845608028654
gelu_cubic = 0.044715
MESH = pl.DeviceIdType.MESH
VMEM_SPEC = pl.BlockSpec(memory_space=pltpu.VMEM)
low = jnp.bfloat16
wide = jnp.float32


def gelu_pair(values):
    square = values * values
    tangent = jnp.tanh(values * (gelu_scale + (gelu_scale * gelu_cubic) * square))
    half = 0.5 + 0.5 * tangent
    bend = values * (0.5 * gelu_scale + (1.5 * gelu_scale * gelu_cubic) * square)
    return values * half, half + bend * (1.0 - tangent * tangent)


def dot(former, latter):
    return jnp.dot(former, latter, preferred_element_type=wide)


def dot_nt(former, latter):
    return lax.dot_general(former, latter, (((1,), (1,)), ((), ())), preferred_element_type=wide)


def dot_tn(former, latter):
    return lax.dot_general(former, latter, (((0,), (0,)), ((), ())), preferred_element_type=wide)


def halves(values):
    high = values.astype(low)
    return high, (values - high.astype(wide)).astype(low)


def dot_fine(former, latter):
    return sum(dot(part, latter) for part in halves(former))


def dot_nt_fine(former, latter):
    return sum(dot_nt(part, latter) for part in halves(former))


def dot_tn_fine(former, latter):
    high, rest = halves(former)
    other, other_rest = halves(latter)
    return dot_tn(high, other) + dot_tn(high, other_rest) + dot_tn(rest, other)


def basis_table(mode_count, length):
    phase = np.outer(np.arange(mode_count), np.arange(length)) % length
    angles = phase * (2.0 * math.pi / length)
    return np.concatenate([np.cos(angles), -np.sin(angles)], axis=0).astype(np.float32)


def analyse(block, first, step, xback_ref, yback_ref, row_ref, column_ref, pool_ref):
    rows, columns, channels = block.shape
    for pair in range(columns // TILE // 2):
        sides = []
        for tile in (2 * pair, 2 * pair + 1):
            piece = block[:, tile * TILE : (tile + 1) * TILE, :]
            sides.append(piece.reshape(rows * TILE, channels).astype(low))
        part = dot(xback_ref[...], jnp.concatenate(sides, axis=1))
        for side in range(2):
            own = pl.ds((2 * pair + side) * TILE, TILE)
            mine = part[:, side * channels : (side + 1) * channels]
            mine = mine.reshape(2 * MODES_X, TILE, channels)

            @pl.when(first)
            def _():
                row_ref[:, own, :] = mine

            @pl.when(jnp.logical_not(first))
            def _():
                row_ref[:, own, :] += mine

    for pair in range(rows // TILE // 2):
        sides = []
        for tile in (2 * pair, 2 * pair + 1):
            piece = block[tile * TILE : (tile + 1) * TILE].reshape(TILE * columns, channels)
            sides.append(piece.astype(low))
        part = dot(yback_ref[...], jnp.concatenate(sides, axis=1))
        for side in range(2):
            own = pl.ds((2 * pair + side) * TILE, TILE)
            mine = part[:, side * channels : (side + 1) * channels]
            column_ref[:, own, :] = mine.reshape(2 * MODES_Y, TILE, channels)
    pooled = block.sum(axis=0).reshape(columns // POOL, POOL, channels).sum(axis=1)
    pool_ref[:, pl.ds(step, 1), :] = pooled[:, None, :]


def analysis_kernel(cells_ref, xback_ref, yback_ref, row_ref, column_ref, pool_ref):
    step = pl.program_id(0)
    block = cells_ref[...].astype(wide)
    analyse(block, step == 0, step, xback_ref, yback_ref, row_ref, column_ref, pool_ref)


def synthesise(rows, columns, channels, xfore, yfore_ref, row_low, column_of, coarse_of):
    parts = []
    for pair in range(rows // TILE // 2):
        sides = []
        for tile in (2 * pair, 2 * pair + 1):
            modes = column_of(tile).reshape(2 * MODES_Y * TILE, channels)
            sides.append(modes.astype(low))
        both = dot(yfore_ref[...], jnp.concatenate(sides, axis=1))
        for side in range(2):
            mine = both[:, side * channels : (side + 1) * channels]
            parts.append(mine.reshape(TILE, columns, channels))
    field = jnp.concatenate(parts, axis=0)
    pieces = []
    for pair in range(columns // TILE // 2):
        both = dot(xfore, row_low(pair))
        for side in range(2):
            mine = both[:, side * channels : (side + 1) * channels]
            part = mine.reshape(rows, TILE, channels)
            pieces.append(part + coarse_of((2 * pair + side) * TILE // POOL))
    return field + jnp.concatenate(pieces, axis=1)


def fill_low(low_ref, tile_of, columns, channels):
    for tile in range(columns // TILE):
        lanes = slice(tile % 2 * channels, (tile % 2 + 1) * channels)
        modes = tile_of(tile).reshape(2 * MODES_X * TILE, channels)
        low_ref[tile // 2, :, lanes] = modes.astype(low)


def ffn_kernel(
    cotangent_ref,
    rowf_ref,
    colf_ref,
    coarse_ref,
    lift_ref,
    liftt_ref,
    dropt_ref,
    xfore_ref,
    xback_ref,
    yfore_ref,
    yback_ref,
    row_ref,
    column_ref,
    pool_ref,
    total_ref,
    rowlow_ref,
):
    step = pl.program_id(0)
    rows, columns, channels = cotangent_ref.shape
    hidden = lift_ref.shape[1]

    @pl.when(step == 0)
    def _():
        fill_low(
            rowlow_ref,
            lambda tile: rowf_ref[:, tile * TILE : (tile + 1) * TILE, :],
            columns,
            channels,
        )
        total_ref[...] = jnp.zeros_like(total_ref)

    coarse = coarse_ref[:, pl.ds(step, 1), :]
    summed = synthesise(
        rows,
        columns,
        channels,
        xfore_ref[...],
        yfore_ref,
        lambda pair: rowlow_ref[pair],
        lambda tile: colf_ref[:, tile * TILE : (tile + 1) * TILE, :],
        lambda place: coarse[place : place + 1],
    )
    count = rows * columns
    entering = summed.reshape(count, channels).astype(low)
    cotangent = cotangent_ref[...].reshape(count, channels)
    before = dot(entering, lift_ref[...])
    value, slope = gelu_pair(before)
    after_grad = dot(cotangent, dropt_ref[...])
    before_grad = (after_grad * slope).astype(low)
    total_ref[:, 0:hidden] += dot_tn(entering, before_grad)
    total_ref[:, hidden : 2 * hidden] += dot_tn(cotangent, value.astype(low))
    back = dot(before_grad, liftt_ref[...]).reshape(rows, columns, channels)
    analyse(back, step == 0, step, xback_ref, yback_ref, row_ref, column_ref, pool_ref)


def greet(sizes):
    barrier = pltpu.get_barrier_semaphore()
    count = 0
    for axis, size in sizes:
        me = lax.axis_index(axis)
        for k in range(1, size):
            pl.semaphore_signal(
                barrier, inc=1, device_id={axis: lax.rem(me + k, size)}, device_id_type=MESH
            )
            count += 1
    pl.semaphore_wait(barrier, count)


def send(axis, size, source_of, target_of, sems):
    me = lax.axis_index(axis)
    copies = []
    for k in range(1, size):
        dest = lax.rem(me + k, size)
        copy = pltpu.make_async_remote_copy(
            src_ref=source_of(dest),
            dst_ref=target_of(k - 1),
            send_sem=sems.at[0, k - 1],
            recv_sem=sems.at[1, k - 1],
            device_id={axis: dest},
            device_id_type=MESH,
        )
        copy.start()
        copies.append(copy)
    return copies


def arrive(copies):
    for copy in copies:
        copy.wait_recv()


def leave(copies):
    for copy in copies:
        copy.wait_send()


def sum_slots(own, slots_ref):
    for k in range(slots_ref.shape[0]):
        own = own + slots_ref[k]
    return own


def share(index, extent):
    return pl.ds(pl.multiple_of(index * extent, extent), extent)


def gy_chain(m, part_ref, slots, full_ref, sem_sum, sem_back, mix_piece, between):
    place = lax.axis_index("gy")
    count = slots.shape[1]
    extent = slots.shape[4]
    half = count * extent
    last = m - 1
    end = (place == 0) | (place == last)

    def piece(side, index):
        begin = side * half + index * extent
        if not isinstance(begin, int):
            begin = pl.multiple_of(begin, extent)
        return pl.ds(begin, extent)

    def forth(side, index, source, dest):
        return pltpu.make_async_remote_copy(
            src_ref=source,
            dst_ref=slots.at[side, index],
            send_sem=sem_sum.at[0, side, index],
            recv_sem=sem_sum.at[1, side, index],
            device_id={"gy": dest},
            device_id_type=MESH,
        )

    def back(side, index, dest):
        return pltpu.make_async_remote_copy(
            src_ref=full_ref.at[:, :, piece(side, index)],
            dst_ref=full_ref.at[:, :, piece(side, index)],
            send_sem=sem_back.at[0, side, index],
            recv_sem=sem_back.at[1, side, index],
            device_id={"gy": dest},
            device_id_type=MESH,
        )

    other = lax.rem(place + 1, m)
    for side in range(2):
        begin = last if side == 0 else 0

        @pl.when(place == begin)
        def _():
            for index in range(count):
                forth(
                    side,
                    index,
                    part_ref.at[:, :, piece(side, index)],
                    last - 1 if side == 0 else 1,
                ).start()

    lag = 3
    for turn in range(count + lag):
        if turn < count:

            @pl.when(jnp.logical_not(end))
            def _():
                for side in (1, 0):
                    forth(side, turn, slots.at[side, turn], other).wait_recv()
                    slots[side, turn] += part_ref[:, :, piece(side, turn)]
                    dest = place + 1 if side else place - 1
                    forth(side, turn, slots.at[side, turn], dest).start()

            @pl.when(end)
            def _():
                side = place // last
                forth(side, turn, slots.at[side, turn], other).wait_recv()
                mix_piece(side, turn, piece(side, turn))
                back(side, turn, 1 + side * (m - 3)).start()

        if turn >= lag:

            @pl.when(jnp.logical_not(end))
            def _():
                index = turn - lag
                for side in (1, 0):
                    back(side, index, other).wait_recv()
                    dest = place - 1 if side else place + 1
                    back(side, index, dest).start()

        between(turn)

    def finish():
        for side in range(2):

            @pl.when(place == (last if side == 0 else 0))
            def _():
                for index in range(count):
                    back(side, index, other).wait_recv()

    def settle():
        for side in range(2):
            final = 0 if side == 0 else last

            @pl.when(place != final)
            def _():
                for index in range(count):
                    forth(side, index, slots.at[side, index], other).wait_send()

            @pl.when(place != last - final)
            def _():
                for index in range(count):
                    back(side, index, other).wait_send()

    return finish, settle


def forward_kernel(
    n,
    m,
    scales,
    rowp_ref,
    colp_ref,
    poolp_ref,
    xweight_ref,
    yweight_ref,
    cweight_ref,
    mixrows_ref,
    rowown_ref,
    colown_ref,
    rowf_ref,
    colf_ref,
    pooled_ref,
    coarse_ref,
    rowslots,
    colslots,
    sem_row,
    sem_col,
    sem_pool,
    sem_rowf,
    sem_colf,
):
    scale_rows, scale_columns = scales
    px, py = lax.axis_index("gx"), lax.axis_index("gy")
    modes = MODES_X // n
    columns, channels = rowp_ref.shape[2:]
    width = poolp_ref.shape[0]
    greet((("gx", n), ("gy", m)))
    to_row = send(
        "gx", n, lambda d: rowp_ref.at[:, share(d, modes)], lambda k: rowslots.at[k], sem_row
    )
    to_pool = send(
        "gy", m, lambda d: poolp_ref, lambda k: pooled_ref.at[share(py, width)], sem_pool
    )
    pooled_ref[share(py, width)] = poolp_ref[...]

    to_rowf = []

    def mix_rows():
        arrive(to_row)
        spec = sum_slots(rowp_ref[:, share(px, modes)], rowslots) * scale_rows
        rowown_ref[...] = spec
        for mode in range(modes):
            both = spec[:, mode].reshape(2 * columns, channels)
            one = dot_fine(both, xweight_ref[0, mode])
            two = dot_fine(both, xweight_ref[1, mode])
            gain = 1.0 / math.sqrt(MODES_X)
            rowf_ref[0, px * modes + mode] = (one[:columns] - two[columns:]) * gain
            rowf_ref[1, px * modes + mode] = (two[:columns] + one[columns:]) * gain
        to_rowf.extend(
            send(
                "gx",
                n,
                lambda d: rowf_ref.at[:, share(px, modes)],
                lambda k: rowf_ref.at[:, share(px, modes)],
                sem_rowf,
            )
        )

    def mix_piece(side, turn, own):
        extent = colslots.shape[4]
        spec = (colslots[side, turn] + colp_ref[:, :, own]) * scale_columns
        colown_ref[:, :, turn * extent : (turn + 1) * extent] = spec
        gain = 1.0 / math.sqrt(MODES_Y)
        for mode in range(MODES_Y):
            both = spec[:, mode].reshape(2 * extent, channels)
            one = dot_fine(both, yweight_ref[0, mode])
            two = dot_fine(both, yweight_ref[1, mode])
            colf_ref[0, mode, own] = (one[:extent] - two[extent:]) * gain
            colf_ref[1, mode, own] = (two[:extent] + one[extent:]) * gain

    def between(turn):
        if turn == 1:
            mix_rows()

    finish, settle = gy_chain(
        m, colp_ref, colslots, colf_ref, sem_col, sem_colf, mix_piece, between
    )

    arrive(to_pool)
    total_width, coarse_rows = pooled_ref.shape[:2]
    pooled = pooled_ref[...].reshape(total_width * coarse_rows, channels) * (1.0 / POOL)
    pre = dot_fine(pooled, cweight_ref[...])
    act, _ = gelu_pair(pre)
    coarse_ref[...] = sum(dot(mixrows_ref[...], part) for part in halves(act)).reshape(coarse_ref.shape)

    arrive(to_rowf)
    finish()
    settle()
    for copies in (to_row, to_pool, to_rowf):
        leave(copies)


def backward_kernel(
    n,
    m,
    scales,
    cotangent_ref,
    rowp_ref,
    colp_ref,
    poolp_ref,
    total_ref,
    rowown_ref,
    colown_ref,
    pooled_ref,
    xweight_ref,
    yweight_ref,
    cweight_ref,
    mixback_ref,
    xfore_ref,
    yfore_ref,
    cell_ref,
    totalf_ref,
    xgrad_ref,
    ygrad_ref,
    cgrad_ref,
    rowslots,
    colslots,
    rowf_ref,
    colf_ref,
    colgrad_ref,
    grads_ref,
    pregrad_ref,
    poolgrad_ref,
    totalslots,
    totalall,
    xpart,
    xslots,
    ypart,
    yslots,
    ychunk,
    ycslots,
    cpart,
    cslots,
    rowlow_ref,
    sem_row,
    sem_col,
    sem_pool,
    sem_rowf,
    sem_colf,
    sem_t,
    sem_tg,
    sem_tf,
    sem_x,
    sem_xf,
    sem_y,
    sem_yc,
    sem_ycf,
    sem_yf,
    sem_c,
    sem_cf,
):
    scale_rows, scale_columns = scales
    px, py = lax.axis_index("gx"), lax.axis_index("gy")
    modes = MODES_X // n
    columns, channels = rowp_ref.shape[2:]
    width, coarse_rows = poolp_ref.shape[:2]
    greet((("gx", n), ("gy", m)))
    to_pool = send(
        "gy", m, lambda d: poolp_ref, lambda k: grads_ref.at[share(py, width)], sem_pool
    )
    to_row = send(
        "gx", n, lambda d: rowp_ref.at[:, share(d, modes)], lambda k: rowslots.at[k], sem_row
    )
    trows = total_ref.shape[0] // n
    grads_ref[share(py, width)] = poolp_ref[...]

    to_c_list = []
    crows = cpart.shape[0] // n

    def coarse_level():
        arrive(to_pool)
        total_width = grads_ref.shape[0]
        count = total_width * coarse_rows
        pooled = pooled_ref[...].reshape(count, channels) * (1.0 / POOL)
        pre = dot_fine(pooled, cweight_ref[...])
        act, slope = gelu_pair(pre)
        grads = grads_ref[...].reshape(count, channels).astype(low)
        pre_grad = dot(mixback_ref[...], grads) * slope
        pregrad_ref[...] = pre_grad.reshape(pregrad_ref.shape)
        cpart[:, 0:channels] = dot_tn_fine(pooled, pre_grad)
        cross = dot_nt(grads, act.astype(low))
        left = lax.broadcasted_iota(jnp.int32, (count, count), 0) % coarse_rows
        right = lax.broadcasted_iota(jnp.int32, (count, count), 1) % coarse_rows
        cross = jnp.where(left == right, cross, 0.0)
        pick = (
            lax.broadcasted_iota(jnp.int32, (channels, count), 0)
            == lax.broadcasted_iota(jnp.int32, (channels, count), 1) // coarse_rows
        ).astype(wide)
        highest = lax.Precision.HIGHEST
        half = jnp.dot(pick, cross, precision=highest, preferred_element_type=wide)
        cpart[:, channels : 2 * channels] = lax.dot_general(
            half, pick, (((1,), (1,)), ((), ())), precision=highest, preferred_element_type=wide
        )
        to_c_list.extend(
            send("gx", n, lambda d: cpart.at[share(d, crows)], lambda k: cslots.at[k], sem_c)
        )
        own_grad = pregrad_ref[share(py, width)].reshape(width * coarse_rows, channels)
        poolgrad_ref[...] = (dot_nt_fine(own_grad, cweight_ref[...]) * (1.0 / POOL)).reshape(
            poolgrad_ref.shape
        )

    def turn_modes(grad):
        size = grad.shape[0] // 2
        return grad, jnp.concatenate([grad[size:], -grad[:size]], axis=0)

    def mix_back(spec, grad, real_weight, imaginary_weight):
        grad, turned = turn_modes(grad)
        back = dot_nt_fine(grad, real_weight) + dot_nt_fine(turned, imaginary_weight)
        return dot_tn_fine(spec, grad), dot_tn_fine(spec, turned), back

    to_rowf, to_t = [], []

    def back_rows():
        arrive(to_row)
        grad = sum_slots(rowp_ref[:, share(px, modes)], rowslots) * (1.0 / math.sqrt(MODES_X))
        for mode in range(modes):
            real, imaginary, back = mix_back(
                rowown_ref[:, mode].reshape(2 * columns, channels),
                grad[:, mode].reshape(2 * columns, channels),
                xweight_ref[0, mode],
                xweight_ref[1, mode],
            )
            xpart[pl.ds(mode * channels, channels)] = real
            xpart[pl.ds((modes + mode) * channels, channels)] = imaginary
            rowf_ref[0, px * modes + mode] = back[:columns] * scale_rows
            rowf_ref[1, px * modes + mode] = back[columns:] * scale_rows
        to_rowf.extend(
            send(
                "gx",
                n,
                lambda d: rowf_ref.at[:, share(px, modes)],
                lambda k: rowf_ref.at[:, share(px, modes)],
                sem_rowf,
            )
        )
        to_t.extend(
            send(
                "gx", n, lambda d: total_ref.at[share(d, trows)], lambda k: totalslots.at[k], sem_t
            )
        )

    extent = colslots.shape[4]

    def mix_piece(side, turn, own):
        grad = (colslots[side, turn] + colp_ref[:, :, own]) * (1.0 / math.sqrt(MODES_Y))
        colgrad_ref[:, :, turn * extent : (turn + 1) * extent] = grad
        for mode in range(MODES_Y):
            both, turned = turn_modes(grad[:, mode].reshape(2 * extent, channels))
            back = dot_nt_fine(both, yweight_ref[0, mode])
            back = back + dot_nt_fine(turned, yweight_ref[1, mode])
            colf_ref[0, mode, own] = back[:extent] * scale_columns
            colf_ref[1, mode, own] = back[extent:] * scale_columns

    def between(turn):
        if turn == 0:
            coarse_level()
        if turn == 1:
            back_rows()

    finish, settle = gy_chain(
        m, colp_ref, colslots, colf_ref, sem_col, sem_colf, mix_piece, between
    )
    to_c = to_c_list
    owner = (py == 0) | (py == m - 1)

    @pl.when(owner)
    def _():
        size = colown_ref.shape[2]
        for mode in range(MODES_Y):
            spec = colown_ref[:, mode].reshape(2 * size, channels)
            grad, turned = turn_modes(colgrad_ref[:, mode].reshape(2 * size, channels))
            ypart[pl.ds(mode * channels, channels)] = dot_tn_fine(spec, grad)
            ypart[pl.ds((MODES_Y + mode) * channels, channels)] = dot_tn_fine(spec, turned)

    @pl.when(jnp.logical_not(owner))
    def _():
        ypart[...] = jnp.zeros_like(ypart)

    yrows = ypart.shape[0] // n
    to_y = send("gx", n, lambda d: ypart.at[share(d, yrows)], lambda k: yslots.at[k], sem_y)
    xrows = xpart.shape[0] // m
    to_x = send("gy", m, lambda d: xpart.at[share(d, xrows)], lambda k: xslots.at[k], sem_x)

    arrive(to_t)
    totalall[py] = sum_slots(total_ref[share(px, trows)], totalslots)
    to_tg = send("gy", m, lambda d: totalall.at[py], lambda k: totalall.at[py], sem_tg)
    arrive(to_c)
    cgrad_ref[share(px, crows)] = sum_slots(cpart[share(px, crows)], cslots)
    to_cf = send(
        "gx",
        n,
        lambda d: cgrad_ref.at[share(px, crows)],
        lambda k: cgrad_ref.at[share(px, crows)],
        sem_cf,
    )

    block = POOL

    def field(step):
        xfore = xfore_ref[pl.ds(pl.multiple_of(step * (block * TILE), block * TILE), block * TILE)]
        coarse = poolgrad_ref[:, pl.ds(step, 1), :]

        def column_of(tile):
            begin = pl.multiple_of(step * block + tile * TILE, TILE)
            return colf_ref[:, :, pl.ds(begin, TILE), :]

        got = synthesise(
            block,
            columns,
            channels,
            xfore,
            yfore_ref,
            lambda pair: rowlow_ref[pair],
            column_of,
            lambda place: coarse[place : place + 1],
        )
        own = pl.ds(pl.multiple_of(step * block, block), block)
        cell_ref[own] = (cotangent_ref[own].astype(wide) + got).astype(low)

    arrive(to_rowf)
    fill_low(
        rowlow_ref,
        lambda tile: rowf_ref[:, :, tile * TILE : (tile + 1) * TILE, :],
        columns,
        channels,
    )
    arrive(to_y)
    ychunk[...] = sum_slots(ypart[share(px, yrows)], yslots)
    ycrows = yrows // m
    to_yc = send("gy", m, lambda d: ychunk.at[share(d, ycrows)], lambda k: ycslots.at[k], sem_yc)
    arrive(to_x)
    xgrad_ref[share(py, xrows)] = sum_slots(xpart[share(py, xrows)], xslots)
    to_xf = send(
        "gy",
        m,
        lambda d: xgrad_ref.at[share(py, xrows)],
        lambda k: xgrad_ref.at[share(py, xrows)],
        sem_xf,
    )
    arrive(to_tg)
    whole_total = totalall[0]
    for k in range(1, m):
        whole_total = whole_total + totalall[k]
    totalf_ref[share(px, trows)] = whole_total
    to_tf = send(
        "gx",
        n,
        lambda d: totalf_ref.at[share(px, trows)],
        lambda k: totalf_ref.at[share(px, trows)],
        sem_tf,
    )
    finish()
    steps = cell_ref.shape[0] // block
    early = steps // 2

    @pl.loop(0, early)
    def _(step):
        field(step)

    arrive(to_yc)
    own_y = pl.ds(pl.multiple_of(px * yrows + py * ycrows, ycrows), ycrows)
    ygrad_ref[own_y] = sum_slots(ychunk[share(py, ycrows)], ycslots)
    to_ycf = send("gy", m, lambda d: ygrad_ref.at[own_y], lambda k: ygrad_ref.at[own_y], sem_ycf)
    arrive(to_ycf)
    to_yf = send(
        "gx",
        n,
        lambda d: ygrad_ref.at[share(px, yrows)],
        lambda k: ygrad_ref.at[share(px, yrows)],
        sem_yf,
    )

    @pl.loop(early, steps)
    def _(step):
        field(step)

    settle()
    for copies in (to_cf, to_xf, to_tf, to_yf):
        arrive(copies)
    for copies in (
        to_pool,
        to_row,
        to_t,
        to_c,
        to_rowf,
        to_y,
        to_x,
        to_tg,
        to_cf,
        to_yc,
        to_xf,
        to_tf,
        to_ycf,
        to_yf,
    ):
        leave(copies)


def spread(rows, columns, row_of, column_of, table, keep):
    left = (
        row_of(lax.broadcasted_iota(jnp.int32, (rows, table.shape[0]), 0))
        == lax.broadcasted_iota(jnp.int32, (rows, table.shape[0]), 1)
    ).astype(low)
    right = (
        column_of(lax.broadcasted_iota(jnp.int32, (table.shape[1], columns), 1))
        == lax.broadcasted_iota(jnp.int32, (table.shape[1], columns), 0)
    ).astype(low)
    full = dot(dot(left, table).astype(low), right)
    place_row = lax.broadcasted_iota(jnp.int32, (rows, columns), 0)
    place_column = lax.broadcasted_iota(jnp.int32, (rows, columns), 1)
    return jnp.where(keep(place_row, place_column), full, 0.0).astype(low)


def remote(size):
    return pltpu.SemaphoreType.DMA((2, size - 1))


def chained():
    return pltpu.SemaphoreType.DMA((2, 2, PIECES))


def on_device(
    n,
    m,
    cells,
    cotangent,
    lift_weight,
    drop_weight,
    xmode_weight,
    ymode_weight,
    coarse_weight,
    coarse_mix,
):
    rows, columns, channels = cells.shape
    hidden = lift_weight.shape[1]
    row_total, column_total = rows * n, columns * m
    coarse_rows, width = rows // POOL, columns // POOL
    total_width = width * m
    modes = MODES_X // n
    px, py = lax.axis_index("gx"), lax.axis_index("gy")
    row_basis = lax.dynamic_slice_in_dim(
        jnp.asarray(basis_table(MODES_X, row_total)), px * rows, rows, 1
    ).astype(low)
    column_basis = lax.dynamic_slice_in_dim(
        jnp.asarray(basis_table(MODES_Y, column_total)), py * columns, columns, 1
    ).astype(low)
    by_tile = lambda v: v // TILE
    same_tile = lambda r, c: r % TILE == c % TILE
    xfore = spread(rows * TILE, 2 * MODES_X * TILE, by_tile, by_tile, row_basis.T, same_tile)
    xback = spread(2 * MODES_X * TILE, rows * TILE, by_tile, by_tile, row_basis, same_tile)
    in_columns = lambda v: v % columns
    yfore = spread(
        TILE * columns,
        2 * MODES_Y * TILE,
        in_columns,
        by_tile,
        column_basis.T,
        lambda r, c: r // columns == c % TILE,
    )
    yback = spread(
        2 * MODES_Y * TILE,
        TILE * columns,
        by_tile,
        in_columns,
        column_basis,
        lambda r, c: r % TILE == c // columns,
    )
    by_coarse = lambda v: v // coarse_rows
    same_coarse = lambda r, c: r % coarse_rows == c % coarse_rows
    mix_rows = lax.dynamic_slice_in_dim(coarse_mix, py * width, width, 0)
    mix_fore = spread(
        width * coarse_rows, total_width * coarse_rows, by_coarse, by_coarse, mix_rows, same_coarse
    )
    mix_back = spread(
        total_width * coarse_rows,
        total_width * coarse_rows,
        by_coarse,
        by_coarse,
        coarse_mix.T,
        same_coarse,
    )
    steps = rows // POOL
    block_spec = pl.BlockSpec((POOL, columns, channels), lambda i: (i, 0, 0))

    def whole(*shape):
        return pl.BlockSpec(shape, lambda i: (0,) * len(shape))

    xback_spec = pl.BlockSpec((2 * MODES_X * TILE, POOL * TILE), lambda i: (0, i))
    xfore_spec = pl.BlockSpec((POOL * TILE, 2 * MODES_X * TILE), lambda i: (i, 0))
    column_spec = pl.BlockSpec((2 * MODES_Y, POOL, channels), lambda i: (0, i, 0))
    analysis_out = [
        jax.ShapeDtypeStruct((2 * MODES_X, columns, channels), wide),
        jax.ShapeDtypeStruct((2 * MODES_Y, rows, channels), wide),
        jax.ShapeDtypeStruct((width, coarse_rows, channels), wide),
    ]
    analysis_specs = [
        whole(2 * MODES_X, columns, channels),
        column_spec,
        whole(width, coarse_rows, channels),
    ]
    sequential = pltpu.CompilerParams(dimension_semantics=("arbitrary",))
    row_part, column_part, pool_part = pl.pallas_call(
        analysis_kernel,
        grid=(steps,),
        in_specs=[block_spec, xback_spec, whole(*yback.shape)],
        out_specs=analysis_specs,
        out_shape=analysis_out,
        compiler_params=sequential,
        name="analysis",
    )(cells, xback, yback)

    scales = (1.0 / math.sqrt(row_total), 1.0 / math.sqrt(column_total))
    row_shape = (2, MODES_X, columns, channels)
    column_shape = (2, MODES_Y, rows, channels)
    f32 = lambda *shape: jax.ShapeDtypeStruct(shape, wide)
    vm = lambda *shape: pltpu.VMEM(shape, wide)
    row_own, column_own, row_full, column_full, pooled, coarse_own = pl.pallas_call(
        functools.partial(forward_kernel, n, m, scales),
        out_shape=[
            f32(2, modes, columns, channels),
            f32(2, MODES_Y, rows // 2, channels),
            f32(*row_shape),
            f32(*column_shape),
            f32(total_width, coarse_rows, channels),
            f32(width, coarse_rows, channels),
        ],
        in_specs=[VMEM_SPEC] * 7,
        out_specs=[VMEM_SPEC] * 6,
        scratch_shapes=[
            vm(n - 1, 2, modes, columns, channels),
            vm(2, PIECES, 2, MODES_Y, rows // 2 // PIECES, channels),
            remote(n),
            chained(),
            remote(m),
            remote(n),
            chained(),
        ],
        compiler_params=pltpu.CompilerParams(collective_id=0, has_side_effects=True),
        name="forward_exchange",
    )(
        row_part.reshape(row_shape),
        column_part.reshape(column_shape),
        pool_part,
        xmode_weight,
        ymode_weight,
        coarse_weight,
        mix_fore,
    )

    row_back, column_back, pool_back, totals = pl.pallas_call(
        ffn_kernel,
        grid=(steps,),
        in_specs=[
            block_spec,
            whole(2 * MODES_X, columns, channels),
            column_spec,
            whole(width, coarse_rows, channels),
            whole(channels, hidden),
            whole(hidden, channels),
            whole(channels, hidden),
            xfore_spec,
            xback_spec,
            whole(*yfore.shape),
            whole(*yback.shape),
        ],
        out_specs=analysis_specs + [whole(channels, 2 * hidden)],
        out_shape=analysis_out + [f32(channels, 2 * hidden)],
        scratch_shapes=[pltpu.VMEM((columns // TILE // 2, 2 * MODES_X * TILE, 2 * channels), low)],
        compiler_params=sequential,
        name="feed_forward",
    )(
        cotangent,
        row_full.reshape(2 * MODES_X, columns, channels),
        column_full.reshape(2 * MODES_Y, rows, channels),
        coarse_own,
        lift_weight,
        lift_weight.T,
        drop_weight.T,
        xfore,
        xback,
        yfore,
        yback,
    )

    trows = channels // n
    xrows = 2 * modes * channels
    yrows = 2 * MODES_Y * channels
    cell_grad, total_full, x_grad, y_grad, c_grad = pl.pallas_call(
        functools.partial(backward_kernel, n, m, scales),
        out_shape=[
            jax.ShapeDtypeStruct(cells.shape, low),
            f32(channels, 2 * hidden),
            f32(xrows, channels),
            f32(yrows, channels),
            f32(channels, 2 * channels),
        ],
        in_specs=[VMEM_SPEC] * 14,
        out_specs=[VMEM_SPEC] * 5,
        scratch_shapes=[
            vm(n - 1, 2, modes, columns, channels),
            vm(2, PIECES, 2, MODES_Y, rows // 2 // PIECES, channels),
            vm(*row_shape),
            vm(*column_shape),
            vm(2, MODES_Y, rows // 2, channels),
            vm(total_width, coarse_rows, channels),
            vm(total_width, coarse_rows, channels),
            vm(width, coarse_rows, channels),
            vm(n - 1, trows, 2 * hidden),
            vm(m, trows, 2 * hidden),
            vm(xrows, channels),
            vm(m - 1, xrows // m, channels),
            vm(yrows, channels),
            vm(n - 1, yrows // n, channels),
            vm(yrows // n, channels),
            vm(m - 1, yrows // n // m, channels),
            vm(channels, 2 * channels),
            vm(n - 1, trows, 2 * channels),
            pltpu.VMEM((columns // TILE // 2, 2 * MODES_X * TILE, 2 * channels), low),
            remote(n),
            chained(),
            remote(m),
            remote(n),
            chained(),
            remote(n),
            remote(m),
            remote(n),
            remote(m),
            remote(m),
            remote(n),
            remote(m),
            remote(m),
            remote(n),
            remote(n),
            remote(n),
        ],
        compiler_params=pltpu.CompilerParams(collective_id=1, has_side_effects=True),
        name="backward_exchange",
    )(
        cotangent,
        row_back.reshape(row_shape),
        column_back.reshape(column_shape),
        pool_back,
        totals,
        row_own,
        column_own,
        pooled,
        xmode_weight,
        ymode_weight,
        coarse_weight,
        mix_back,
        xfore,
        yfore,
    )
    return (
        cell_grad,
        total_full[:, :hidden],
        total_full[:, hidden:].T,
        x_grad.reshape(2, modes, channels, channels),
        y_grad.reshape(2, MODES_Y, channels, channels),
        c_grad[:, :channels],
        c_grad[:total_width, channels : channels + total_width],
    )


def solution(mesh):
    in_specs = (
        P("gx", "gy", None),
        P("gx", "gy", None),
        P(),
        P(),
        P(None, "gx", None, None),
        P(),
        P(),
        P(),
    )
    out_specs = (P("gx", "gy", None), P(), P(), P(None, "gx", None, None), P(), P(), P())
    return jax.shard_map(
        functools.partial(on_device, mesh.shape["gx"], mesh.shape["gy"]),
        mesh=mesh,
        in_specs=in_specs,
        out_specs=out_specs,
        check_vma=False,
    )
```

```python
import functools
import math

import jax
import jax.numpy as jnp
import numpy as np
from jax import lax
from jax.experimental import pallas as pl
from jax.experimental.pallas import tpu as pltpu
from jax.sharding import PartitionSpec as P

MODES_X = 16
MODES_Y = 8
POOL = 16
TILE = 8

gelu_scale = 0.7978845608028654
gelu_cubic = 0.044715
MESH = pl.DeviceIdType.MESH
VMEM_SPEC = pl.BlockSpec(memory_space=pltpu.VMEM)
low = jnp.bfloat16
wide = jnp.float32


def gelu_pair(values):
    square = values * values
    tangent = jnp.tanh(values * (gelu_scale + (gelu_scale * gelu_cubic) * square))
    half = 0.5 + 0.5 * tangent
    bend = values * (0.5 * gelu_scale + (1.5 * gelu_scale * gelu_cubic) * square)
    return values * half, half + bend * (1.0 - tangent * tangent)


def dot(former, latter):
    return jnp.dot(former, latter, preferred_element_type=wide)


def dot_nt(former, latter):
    return lax.dot_general(former, latter, (((1,), (1,)), ((), ())), preferred_element_type=wide)


def dot_tn(former, latter):
    return lax.dot_general(former, latter, (((0,), (0,)), ((), ())), preferred_element_type=wide)


def halves(values):
    high = values.astype(low)
    return high, (values - high.astype(wide)).astype(low)


def dot_fine(former, latter):
    return sum(dot(part, latter) for part in halves(former))


def dot_nt_fine(former, latter):
    return sum(dot_nt(part, latter) for part in halves(former))


def dot_tn_fine(former, latter):
    high, rest = halves(former)
    other, other_rest = halves(latter)
    return dot_tn(high, other) + dot_tn(high, other_rest) + dot_tn(rest, other)


def basis_table(mode_count, length):
    phase = np.outer(np.arange(mode_count), np.arange(length)) % length
    angles = phase * (2.0 * math.pi / length)
    return np.concatenate([np.cos(angles), -np.sin(angles)], axis=0).astype(np.float32)


def analyse(block, first, step, xback_ref, yback_ref, row_ref, column_ref, pool_ref):
    rows, columns, channels = block.shape
    for pair in range(columns // TILE // 2):
        sides = []
        for tile in (2 * pair, 2 * pair + 1):
            piece = block[:, tile * TILE : (tile + 1) * TILE, :]
            sides.append(piece.reshape(rows * TILE, channels).astype(low))
        part = dot(xback_ref[...], jnp.concatenate(sides, axis=1))
        for side in range(2):
            own = pl.ds((2 * pair + side) * TILE, TILE)
            mine = part[:, side * channels : (side + 1) * channels]
            mine = mine.reshape(2 * MODES_X, TILE, channels)

            @pl.when(first)
            def _():
                row_ref[:, own, :] = mine

            @pl.when(jnp.logical_not(first))
            def _():
                row_ref[:, own, :] += mine

    for pair in range(rows // TILE // 2):
        sides = []
        for tile in (2 * pair, 2 * pair + 1):
            piece = block[tile * TILE : (tile + 1) * TILE].reshape(TILE * columns, channels)
            sides.append(piece.astype(low))
        part = dot(yback_ref[...], jnp.concatenate(sides, axis=1))
        for side in range(2):
            own = pl.ds((2 * pair + side) * TILE, TILE)
            mine = part[:, side * channels : (side + 1) * channels]
            column_ref[:, own, :] = mine.reshape(2 * MODES_Y, TILE, channels)
    pooled = block.sum(axis=0).reshape(columns // POOL, POOL, channels).sum(axis=1)
    pool_ref[:, pl.ds(step, 1), :] = pooled[:, None, :]


def analysis_kernel(cells_ref, xback_ref, yback_ref, row_ref, column_ref, pool_ref):
    step = pl.program_id(0)
    block = cells_ref[...].astype(wide)
    analyse(block, step == 0, step, xback_ref, yback_ref, row_ref, column_ref, pool_ref)


def synthesise(rows, columns, channels, xfore, yfore_ref, row_low, column_of, coarse_of):
    parts = []
    for pair in range(rows // TILE // 2):
        sides = []
        for tile in (2 * pair, 2 * pair + 1):
            modes = column_of(tile).reshape(2 * MODES_Y * TILE, channels)
            sides.append(modes.astype(low))
        both = dot(yfore_ref[...], jnp.concatenate(sides, axis=1))
        for side in range(2):
            mine = both[:, side * channels : (side + 1) * channels]
            parts.append(mine.reshape(TILE, columns, channels))
    field = jnp.concatenate(parts, axis=0)
    pieces = []
    for pair in range(columns // TILE // 2):
        both = dot(xfore, row_low(pair))
        for side in range(2):
            mine = both[:, side * channels : (side + 1) * channels]
            part = mine.reshape(rows, TILE, channels)
            pieces.append(part + coarse_of((2 * pair + side) * TILE // POOL))
    return field + jnp.concatenate(pieces, axis=1)


def fill_low(low_ref, tile_of, columns, channels):
    for tile in range(columns // TILE):
        lanes = slice(tile % 2 * channels, (tile % 2 + 1) * channels)
        modes = tile_of(tile).reshape(2 * MODES_X * TILE, channels)
        low_ref[tile // 2, :, lanes] = modes.astype(low)


def ffn_kernel(
    cotangent_ref,
    rowf_ref,
    colf_ref,
    coarse_ref,
    lift_ref,
    liftt_ref,
    dropt_ref,
    xfore_ref,
    xback_ref,
    yfore_ref,
    yback_ref,
    row_ref,
    column_ref,
    pool_ref,
    total_ref,
    rowlow_ref,
):
    step = pl.program_id(0)
    rows, columns, channels = cotangent_ref.shape
    hidden = lift_ref.shape[1]

    @pl.when(step == 0)
    def _():
        fill_low(
            rowlow_ref,
            lambda tile: rowf_ref[:, tile * TILE : (tile + 1) * TILE, :],
            columns,
            channels,
        )
        total_ref[...] = jnp.zeros_like(total_ref)

    coarse = coarse_ref[:, pl.ds(step, 1), :]
    summed = synthesise(
        rows,
        columns,
        channels,
        xfore_ref[...],
        yfore_ref,
        lambda pair: rowlow_ref[pair],
        lambda tile: colf_ref[:, tile * TILE : (tile + 1) * TILE, :],
        lambda place: coarse[place : place + 1],
    )
    count = rows * columns
    entering = summed.reshape(count, channels).astype(low)
    cotangent = cotangent_ref[...].reshape(count, channels)
    before = dot(entering, lift_ref[...])
    value, slope = gelu_pair(before)
    after_grad = dot(cotangent, dropt_ref[...])
    before_grad = (after_grad * slope).astype(low)
    total_ref[:, 0:hidden] += dot_tn(entering, before_grad)
    total_ref[:, hidden : 2 * hidden] += dot_tn(cotangent, value.astype(low))
    back = dot(before_grad, liftt_ref[...]).reshape(rows, columns, channels)
    analyse(back, step == 0, step, xback_ref, yback_ref, row_ref, column_ref, pool_ref)


def greet(sizes):
    barrier = pltpu.get_barrier_semaphore()
    count = 0
    for axis, size in sizes:
        me = lax.axis_index(axis)
        for k in range(1, size):
            pl.semaphore_signal(
                barrier, inc=1, device_id={axis: lax.rem(me + k, size)}, device_id_type=MESH
            )
            count += 1
    pl.semaphore_wait(barrier, count)


def send(axis, size, source_of, target_of, sems):
    me = lax.axis_index(axis)
    copies = []
    for k in range(1, size):
        dest = lax.rem(me + k, size)
        copy = pltpu.make_async_remote_copy(
            src_ref=source_of(dest),
            dst_ref=target_of(k - 1),
            send_sem=sems.at[0, k - 1],
            recv_sem=sems.at[1, k - 1],
            device_id={axis: dest},
            device_id_type=MESH,
        )
        copy.start()
        copies.append(copy)
    return copies


def arrive(copies):
    for copy in copies:
        copy.wait_recv()


def leave(copies):
    for copy in copies:
        copy.wait_send()


def sum_slots(own, slots_ref):
    for k in range(slots_ref.shape[0]):
        own = own + slots_ref[k]
    return own


def share(index, extent):
    return pl.ds(pl.multiple_of(index * extent, extent), extent)


def forward_kernel(
    n,
    m,
    scales,
    rowp_ref,
    colp_ref,
    poolp_ref,
    xweight_ref,
    yweight_ref,
    cweight_ref,
    mixall_ref,
    xback_ref,
    yback_ref,
    rowown_ref,
    colown_ref,
    rowf_ref,
    colf_ref,
    pooled_ref,
    coarse_ref,
    xfore_ref,
    yfore_ref,
    rowslots,
    colslots,
    sem_row,
    sem_col,
    sem_pool,
    sem_rowf,
    sem_colf,
):
    scale_rows, scale_columns = scales
    px, py = lax.axis_index("gx"), lax.axis_index("gy")
    modes = MODES_X // n
    columns, channels = rowp_ref.shape[2:]
    rows = colp_ref.shape[2] // m
    width = poolp_ref.shape[0]
    greet((("gx", n), ("gy", m)))
    to_col = send(
        "gy", m, lambda d: colp_ref.at[:, :, share(d, rows)], lambda k: colslots.at[k], sem_col
    )
    to_row = send(
        "gx", n, lambda d: rowp_ref.at[:, share(d, modes)], lambda k: rowslots.at[k], sem_row
    )
    to_pool = send(
        "gy", m, lambda d: poolp_ref, lambda k: pooled_ref.at[share(py, width)], sem_pool
    )
    pooled_ref[share(py, width)] = poolp_ref[...]
    for back_ref, fore_ref in ((xback_ref, xfore_ref), (yback_ref, yfore_ref)):
        for begin in range(0, back_ref.shape[1], channels):
            part = back_ref[:, begin : begin + channels].astype(wide)
            fore_ref[begin : begin + channels] = part.T.astype(low)

    arrive(to_row)
    spec = sum_slots(rowp_ref[:, share(px, modes)], rowslots) * scale_rows
    rowown_ref[...] = spec
    for mode in range(modes):
        both = spec[:, mode].reshape(2 * columns, channels)
        one = dot_fine(both, xweight_ref[0, mode])
        two = dot_fine(both, xweight_ref[1, mode])
        gain = 1.0 / math.sqrt(MODES_X)
        rowf_ref[0, px * modes + mode] = (one[:columns] - two[columns:]) * gain
        rowf_ref[1, px * modes + mode] = (two[:columns] + one[columns:]) * gain
    to_rowf = send(
        "gx",
        n,
        lambda d: rowf_ref.at[:, share(px, modes)],
        lambda k: rowf_ref.at[:, share(px, modes)],
        sem_rowf,
    )

    arrive(to_col)
    for mode in range(MODES_Y):
        spec = colp_ref[:, mode, share(py, rows)]
        for k in range(m - 1):
            spec = spec + colslots[k, :, mode]
        spec = spec * scale_columns
        colown_ref[:, mode] = spec
        both = spec.reshape(2 * rows, channels)
        one = dot_fine(both, yweight_ref[0, mode])
        two = dot_fine(both, yweight_ref[1, mode])
        gain = 1.0 / math.sqrt(MODES_Y)
        colf_ref[0, mode, share(py, rows)] = (one[:rows] - two[rows:]) * gain
        colf_ref[1, mode, share(py, rows)] = (two[:rows] + one[rows:]) * gain
    to_colf = send(
        "gy",
        m,
        lambda d: colf_ref.at[:, :, share(py, rows)],
        lambda k: colf_ref.at[:, :, share(py, rows)],
        sem_colf,
    )

    arrive(to_pool)
    total_width, coarse_rows = pooled_ref.shape[:2]
    pooled = pooled_ref[...].reshape(total_width * coarse_rows, channels) * (1.0 / POOL)
    pre = dot_fine(pooled, cweight_ref[...])
    act, _ = gelu_pair(pre)
    own_rows = mixall_ref[share(py, width * coarse_rows)]
    coarse_ref[...] = sum(dot(own_rows, part) for part in halves(act)).reshape(coarse_ref.shape)

    arrive(to_rowf)
    arrive(to_colf)
    for copies in (to_row, to_col, to_pool, to_rowf, to_colf):
        leave(copies)


def backward_kernel(
    n,
    m,
    scales,
    cotangent_ref,
    rowp_ref,
    colp_ref,
    poolp_ref,
    total_ref,
    rowown_ref,
    colown_ref,
    pooled_ref,
    xweight_ref,
    yweight_ref,
    cweight_ref,
    mixall_ref,
    xfore_ref,
    yfore_ref,
    cell_ref,
    totalf_ref,
    xgrad_ref,
    ygrad_ref,
    cgrad_ref,
    rowslots,
    colslots,
    rowf_ref,
    colf_ref,
    grads_ref,
    pregrad_ref,
    poolgrad_ref,
    totalslots,
    totalall,
    xpart,
    xslots,
    ypart,
    yslots,
    ychunk,
    ycslots,
    cpart,
    cslots,
    rowlow_ref,
    sem_row,
    sem_col,
    sem_pool,
    sem_rowf,
    sem_colf,
    sem_t,
    sem_tg,
    sem_tf,
    sem_x,
    sem_xf,
    sem_y,
    sem_yc,
    sem_ycf,
    sem_yf,
    sem_c,
    sem_cf,
):
    scale_rows, scale_columns = scales
    px, py = lax.axis_index("gx"), lax.axis_index("gy")
    modes = MODES_X // n
    columns, channels = rowp_ref.shape[2:]
    rows = colp_ref.shape[2] // m
    width, coarse_rows = poolp_ref.shape[:2]
    greet((("gx", n), ("gy", m)))
    to_pool = send(
        "gy", m, lambda d: poolp_ref, lambda k: grads_ref.at[share(py, width)], sem_pool
    )
    to_col = send(
        "gy", m, lambda d: colp_ref.at[:, :, share(d, rows)], lambda k: colslots.at[k], sem_col
    )
    to_row = send(
        "gx", n, lambda d: rowp_ref.at[:, share(d, modes)], lambda k: rowslots.at[k], sem_row
    )
    trows = total_ref.shape[0] // n
    to_t = send(
        "gx", n, lambda d: total_ref.at[share(d, trows)], lambda k: totalslots.at[k], sem_t
    )
    grads_ref[share(py, width)] = poolp_ref[...]

    arrive(to_pool)
    total_width = grads_ref.shape[0]
    count = total_width * coarse_rows
    pooled = pooled_ref[...].reshape(count, channels) * (1.0 / POOL)
    pre = dot_fine(pooled, cweight_ref[...])
    act, slope = gelu_pair(pre)
    grads = grads_ref[...].reshape(count, channels).astype(low)
    pre_grad = dot_tn(mixall_ref[...], grads) * slope
    pregrad_ref[...] = pre_grad.reshape(pregrad_ref.shape)
    cpart[:, 0:channels] = dot_tn_fine(pooled, pre_grad)
    cross = dot_nt(grads, act.astype(low))
    left = lax.broadcasted_iota(jnp.int32, (count, count), 0) % coarse_rows
    right = lax.broadcasted_iota(jnp.int32, (count, count), 1) % coarse_rows
    cross = jnp.where(left == right, cross, 0.0)
    pick = (
        lax.broadcasted_iota(jnp.int32, (channels, count), 0)
        == lax.broadcasted_iota(jnp.int32, (channels, count), 1) // coarse_rows
    ).astype(wide)
    highest = lax.Precision.HIGHEST
    half = jnp.dot(pick, cross, precision=highest, preferred_element_type=wide)
    cpart[:, channels : 2 * channels] = lax.dot_general(
        half, pick, (((1,), (1,)), ((), ())), precision=highest, preferred_element_type=wide
    )
    crows = cpart.shape[0] // n
    to_c = send("gx", n, lambda d: cpart.at[share(d, crows)], lambda k: cslots.at[k], sem_c)
    own_grad = pregrad_ref[share(py, width)].reshape(width * coarse_rows, channels)
    poolgrad_ref[...] = (dot_nt_fine(own_grad, cweight_ref[...]) * (1.0 / POOL)).reshape(
        poolgrad_ref.shape
    )

    def turn_modes(grad):
        half_rows = grad.shape[0] // 2
        return grad, jnp.concatenate([grad[half_rows:], -grad[:half_rows]], axis=0)

    def weight_back(spec, grad):
        grad, turned = turn_modes(grad)
        return dot_tn_fine(spec, grad), dot_tn_fine(spec, turned)

    def spec_back(grad, real_weight, imaginary_weight):
        grad, turned = turn_modes(grad)
        return dot_nt_fine(grad, real_weight) + dot_nt_fine(turned, imaginary_weight)

    arrive(to_row)
    grad = sum_slots(rowp_ref[:, share(px, modes)], rowslots) * (1.0 / math.sqrt(MODES_X))
    for mode in range(modes):
        back = spec_back(
            grad[:, mode].reshape(2 * columns, channels), xweight_ref[0, mode], xweight_ref[1, mode]
        )
        rowf_ref[0, px * modes + mode] = back[:columns] * scale_rows
        rowf_ref[1, px * modes + mode] = back[columns:] * scale_rows
    to_rowf = send(
        "gx",
        n,
        lambda d: rowf_ref.at[:, share(px, modes)],
        lambda k: rowf_ref.at[:, share(px, modes)],
        sem_rowf,
    )
    for mode in range(modes):
        real, imaginary = weight_back(
            rowown_ref[:, mode].reshape(2 * columns, channels),
            grad[:, mode].reshape(2 * columns, channels),
        )
        xpart[pl.ds(mode * channels, channels)] = real
        xpart[pl.ds((modes + mode) * channels, channels)] = imaginary

    arrive(to_col)
    grad = colp_ref[:, :, share(py, rows)]
    for k in range(m - 1):
        grad = grad + colslots[k]
    grad = grad * (1.0 / math.sqrt(MODES_Y))
    for mode in range(MODES_Y):
        real, imaginary = weight_back(
            colown_ref[:, mode].reshape(2 * rows, channels),
            grad[:, mode].reshape(2 * rows, channels),
        )
        ypart[pl.ds(mode * channels, channels)] = real
        ypart[pl.ds((MODES_Y + mode) * channels, channels)] = imaginary
    yrows = ypart.shape[0] // n
    to_y = send("gx", n, lambda d: ypart.at[share(d, yrows)], lambda k: yslots.at[k], sem_y)
    for mode in range(MODES_Y):
        back = spec_back(
            grad[:, mode].reshape(2 * rows, channels), yweight_ref[0, mode], yweight_ref[1, mode]
        )
        colf_ref[0, mode, share(py, rows)] = back[:rows] * scale_columns
        colf_ref[1, mode, share(py, rows)] = back[rows:] * scale_columns
    to_colf = send(
        "gy",
        m,
        lambda d: colf_ref.at[:, :, share(py, rows)],
        lambda k: colf_ref.at[:, :, share(py, rows)],
        sem_colf,
    )
    xrows = xpart.shape[0] // m
    to_x = send("gy", m, lambda d: xpart.at[share(d, xrows)], lambda k: xslots.at[k], sem_x)

    arrive(to_t)
    totalall[py] = sum_slots(total_ref[share(px, trows)], totalslots)
    to_tg = send("gy", m, lambda d: totalall.at[py], lambda k: totalall.at[py], sem_tg)
    arrive(to_c)
    cgrad_ref[share(px, crows)] = sum_slots(cpart[share(px, crows)], cslots)
    to_cf = send(
        "gx",
        n,
        lambda d: cgrad_ref.at[share(px, crows)],
        lambda k: cgrad_ref.at[share(px, crows)],
        sem_cf,
    )

    block = POOL

    def field(step):
        xfore = xfore_ref[pl.ds(pl.multiple_of(step * (block * TILE), block * TILE), block * TILE)]
        coarse = poolgrad_ref[:, pl.ds(step, 1), :]

        def column_of(tile):
            begin = pl.multiple_of(step * block + tile * TILE, TILE)
            return colf_ref[:, :, pl.ds(begin, TILE), :]

        got = synthesise(
            block,
            columns,
            channels,
            xfore,
            yfore_ref,
            lambda pair: rowlow_ref[pair],
            column_of,
            lambda place: coarse[place : place + 1],
        )
        own = pl.ds(pl.multiple_of(step * block, block), block)
        cell_ref[own] = (cotangent_ref[own].astype(wide) + got).astype(low)

    arrive(to_rowf)
    fill_low(
        rowlow_ref,
        lambda tile: rowf_ref[:, :, tile * TILE : (tile + 1) * TILE, :],
        columns,
        channels,
    )
    arrive(to_y)
    ychunk[...] = sum_slots(ypart[share(px, yrows)], yslots)
    ycrows = yrows // m
    to_yc = send("gy", m, lambda d: ychunk.at[share(d, ycrows)], lambda k: ycslots.at[k], sem_yc)
    arrive(to_x)
    xgrad_ref[share(py, xrows)] = sum_slots(xpart[share(py, xrows)], xslots)
    to_xf = send(
        "gy",
        m,
        lambda d: xgrad_ref.at[share(py, xrows)],
        lambda k: xgrad_ref.at[share(py, xrows)],
        sem_xf,
    )
    arrive(to_tg)
    whole_total = totalall[0]
    for k in range(1, m):
        whole_total = whole_total + totalall[k]
    totalf_ref[share(px, trows)] = whole_total
    to_tf = send(
        "gx",
        n,
        lambda d: totalf_ref.at[share(px, trows)],
        lambda k: totalf_ref.at[share(px, trows)],
        sem_tf,
    )
    arrive(to_colf)
    steps = cell_ref.shape[0] // block
    early = steps // 2

    arrive(to_yc)
    own_y = pl.ds(pl.multiple_of(px * yrows + py * ycrows, ycrows), ycrows)
    ygrad_ref[own_y] = sum_slots(ychunk[share(py, ycrows)], ycslots)
    to_ycf = send("gy", m, lambda d: ygrad_ref.at[own_y], lambda k: ygrad_ref.at[own_y], sem_ycf)
    @pl.loop(0, early)
    def _(step):
        field(step)

    arrive(to_ycf)
    to_yf = send(
        "gx",
        n,
        lambda d: ygrad_ref.at[share(px, yrows)],
        lambda k: ygrad_ref.at[share(px, yrows)],
        sem_yf,
    )

    @pl.loop(early, steps)
    def _(step):
        field(step)

    for copies in (to_cf, to_xf, to_tf, to_yf):
        arrive(copies)
    for copies in (
        to_pool,
        to_col,
        to_row,
        to_t,
        to_c,
        to_rowf,
        to_colf,
        to_y,
        to_x,
        to_tg,
        to_cf,
        to_yc,
        to_xf,
        to_tf,
        to_ycf,
        to_yf,
    ):
        leave(copies)


def spread(rows, columns, row_of, column_of, table, keep):
    left = (
        row_of(lax.broadcasted_iota(jnp.int32, (rows, table.shape[0]), 0))
        == lax.broadcasted_iota(jnp.int32, (rows, table.shape[0]), 1)
    ).astype(low)
    right = (
        column_of(lax.broadcasted_iota(jnp.int32, (table.shape[1], columns), 1))
        == lax.broadcasted_iota(jnp.int32, (table.shape[1], columns), 0)
    ).astype(low)
    full = dot(dot(left, table).astype(low), right)
    place_row = lax.broadcasted_iota(jnp.int32, (rows, columns), 0)
    place_column = lax.broadcasted_iota(jnp.int32, (rows, columns), 1)
    return jnp.where(keep(place_row, place_column), full, 0.0).astype(low)


def remote(size):
    return pltpu.SemaphoreType.DMA((2, size - 1))


def on_device(
    n,
    m,
    cells,
    cotangent,
    lift_weight,
    drop_weight,
    xmode_weight,
    ymode_weight,
    coarse_weight,
    coarse_mix,
):
    rows, columns, channels = cells.shape
    hidden = lift_weight.shape[1]
    row_total, column_total = rows * n, columns * m
    coarse_rows, width = rows // POOL, columns // POOL
    total_width = width * m
    modes = MODES_X // n
    row_share = rows // m
    px, py = lax.axis_index("gx"), lax.axis_index("gy")
    row_basis = lax.dynamic_slice_in_dim(
        jnp.asarray(basis_table(MODES_X, row_total)), px * rows, rows, 1
    ).astype(low)
    column_basis = lax.dynamic_slice_in_dim(
        jnp.asarray(basis_table(MODES_Y, column_total)), py * columns, columns, 1
    ).astype(low)
    by_tile = lambda v: v // TILE
    same_tile = lambda r, c: r % TILE == c % TILE
    xback = spread(2 * MODES_X * TILE, rows * TILE, by_tile, by_tile, row_basis, same_tile)
    in_columns = lambda v: v % columns
    yback = spread(
        2 * MODES_Y * TILE,
        TILE * columns,
        by_tile,
        in_columns,
        column_basis,
        lambda r, c: r % TILE == c // columns,
    )
    by_coarse = lambda v: v // coarse_rows
    same_coarse = lambda r, c: r % coarse_rows == c % coarse_rows
    mix_all = spread(
        total_width * coarse_rows,
        total_width * coarse_rows,
        by_coarse,
        by_coarse,
        coarse_mix,
        same_coarse,
    )
    steps = rows // POOL
    block_spec = pl.BlockSpec((POOL, columns, channels), lambda i: (i, 0, 0))

    def whole(*shape):
        return pl.BlockSpec(shape, lambda i: (0,) * len(shape))

    xback_spec = pl.BlockSpec((2 * MODES_X * TILE, POOL * TILE), lambda i: (0, i))
    xfore_spec = pl.BlockSpec((POOL * TILE, 2 * MODES_X * TILE), lambda i: (i, 0))
    column_spec = pl.BlockSpec((2 * MODES_Y, POOL, channels), lambda i: (0, i, 0))
    analysis_out = [
        jax.ShapeDtypeStruct((2 * MODES_X, columns, channels), wide),
        jax.ShapeDtypeStruct((2 * MODES_Y, rows, channels), wide),
        jax.ShapeDtypeStruct((width, coarse_rows, channels), wide),
    ]
    analysis_specs = [
        whole(2 * MODES_X, columns, channels),
        column_spec,
        whole(width, coarse_rows, channels),
    ]
    sequential = pltpu.CompilerParams(dimension_semantics=("arbitrary",))
    row_part, column_part, pool_part = pl.pallas_call(
        analysis_kernel,
        grid=(steps,),
        in_specs=[block_spec, xback_spec, whole(*yback.shape)],
        out_specs=analysis_specs,
        out_shape=analysis_out,
        compiler_params=sequential,
        name="analysis",
    )(cells, xback, yback)

    scales = (1.0 / math.sqrt(row_total), 1.0 / math.sqrt(column_total))
    row_shape = (2, MODES_X, columns, channels)
    column_shape = (2, MODES_Y, rows, channels)
    f32 = lambda *shape: jax.ShapeDtypeStruct(shape, wide)
    vm = lambda *shape: pltpu.VMEM(shape, wide)
    row_own, column_own, row_full, column_full, pooled, coarse_own, xfore, yfore = pl.pallas_call(
        functools.partial(forward_kernel, n, m, scales),
        out_shape=[
            f32(2, modes, columns, channels),
            f32(2, MODES_Y, row_share, channels),
            f32(*row_shape),
            f32(*column_shape),
            f32(total_width, coarse_rows, channels),
            f32(width, coarse_rows, channels),
            jax.ShapeDtypeStruct(xback.shape[::-1], low),
            jax.ShapeDtypeStruct(yback.shape[::-1], low),
        ],
        in_specs=[VMEM_SPEC] * 9,
        out_specs=[VMEM_SPEC] * 8,
        scratch_shapes=[
            vm(n - 1, 2, modes, columns, channels),
            vm(m - 1, 2, MODES_Y, row_share, channels),
            remote(n),
            remote(m),
            remote(m),
            remote(n),
            remote(m),
        ],
        compiler_params=pltpu.CompilerParams(collective_id=0, has_side_effects=True),
        name="forward_exchange",
    )(
        row_part.reshape(row_shape),
        column_part.reshape(column_shape),
        pool_part,
        xmode_weight,
        ymode_weight,
        coarse_weight,
        mix_all,
        xback,
        yback,
    )

    row_back, column_back, pool_back, totals = pl.pallas_call(
        ffn_kernel,
        grid=(steps,),
        in_specs=[
            block_spec,
            whole(2 * MODES_X, columns, channels),
            column_spec,
            whole(width, coarse_rows, channels),
            whole(channels, hidden),
            whole(hidden, channels),
            whole(channels, hidden),
            xfore_spec,
            xback_spec,
            whole(*yfore.shape),
            whole(*yback.shape),
        ],
        out_specs=analysis_specs + [whole(channels, 2 * hidden)],
        out_shape=analysis_out + [f32(channels, 2 * hidden)],
        scratch_shapes=[pltpu.VMEM((columns // TILE // 2, 2 * MODES_X * TILE, 2 * channels), low)],
        compiler_params=sequential,
        name="feed_forward",
    )(
        cotangent,
        row_full.reshape(2 * MODES_X, columns, channels),
        column_full.reshape(2 * MODES_Y, rows, channels),
        coarse_own,
        lift_weight,
        lift_weight.T,
        drop_weight.T,
        xfore,
        xback,
        yfore,
        yback,
    )

    trows = channels // n
    xrows = 2 * modes * channels
    yrows = 2 * MODES_Y * channels
    cell_grad, total_full, x_grad, y_grad, c_grad = pl.pallas_call(
        functools.partial(backward_kernel, n, m, scales),
        out_shape=[
            jax.ShapeDtypeStruct(cells.shape, low),
            f32(channels, 2 * hidden),
            f32(xrows, channels),
            f32(yrows, channels),
            f32(channels, 2 * channels),
        ],
        in_specs=[VMEM_SPEC] * 14,
        out_specs=[VMEM_SPEC] * 5,
        scratch_shapes=[
            vm(n - 1, 2, modes, columns, channels),
            vm(m - 1, 2, MODES_Y, row_share, channels),
            vm(*row_shape),
            vm(*column_shape),
            vm(total_width, coarse_rows, channels),
            vm(total_width, coarse_rows, channels),
            vm(width, coarse_rows, channels),
            vm(n - 1, trows, 2 * hidden),
            vm(m, trows, 2 * hidden),
            vm(xrows, channels),
            vm(m - 1, xrows // m, channels),
            vm(yrows, channels),
            vm(n - 1, yrows // n, channels),
            vm(yrows // n, channels),
            vm(m - 1, yrows // n // m, channels),
            vm(channels, 2 * channels),
            vm(n - 1, trows, 2 * channels),
            pltpu.VMEM((columns // TILE // 2, 2 * MODES_X * TILE, 2 * channels), low),
            remote(n),
            remote(m),
            remote(m),
            remote(n),
            remote(m),
            remote(n),
            remote(m),
            remote(n),
            remote(m),
            remote(m),
            remote(n),
            remote(m),
            remote(m),
            remote(n),
            remote(n),
            remote(n),
        ],
        compiler_params=pltpu.CompilerParams(collective_id=1, has_side_effects=True),
        name="backward_exchange",
    )(
        cotangent,
        row_back.reshape(row_shape),
        column_back.reshape(column_shape),
        pool_back,
        totals,
        row_own,
        column_own,
        pooled,
        xmode_weight,
        ymode_weight,
        coarse_weight,
        mix_all,
        xfore,
        yfore,
    )
    return (
        cell_grad,
        total_full[:, :hidden],
        total_full[:, hidden:].T,
        x_grad.reshape(2, modes, channels, channels),
        y_grad.reshape(2, MODES_Y, channels, channels),
        c_grad[:, :channels],
        c_grad[:total_width, channels : channels + total_width],
    )


def solution(mesh):
    in_specs = (
        P("gx", "gy", None),
        P("gx", "gy", None),
        P(),
        P(),
        P(None, "gx", None, None),
        P(),
        P(),
        P(),
    )
    out_specs = (P("gx", "gy", None), P(), P(), P(None, "gx", None, None), P(), P(), P())
    return jax.shard_map(
        functools.partial(on_device, mesh.shape["gx"], mesh.shape["gy"]),
        mesh=mesh,
        in_specs=in_specs,
        out_specs=out_specs,
        check_vma=False,
    )
```
